32 devices in a mesh: row: 8 (over z, core), col: 4 (over y, x).
Axes of the slice: x: 2, y: 2, z: 4, core: 2. Of those that a mesh axis runs over, the one named last changes fastest.
Arguments:
- features: bfloat16 [9, 1, 128, 128, 128], P(None, None, 'row', 'col'), may hold values from -12 to 12
- cotangent: float32 [3, 1, 128, 128, 128], P(None, None, 'row', 'col'), may hold values from -14 to 14
- w_in: bfloat16 [9, 256], replicated, may hold values from -2 to 2
- bias_in: float32 [256], replicated, may hold values from -3 to 3
- w_mid: bfloat16 [256, 256], replicated, may hold values from -0.375 to 0.375
- bias_mid: float32 [256], replicated, may hold values from -3 to 3
- w_out: bfloat16 [256, 6], replicated, may hold values from -2.5 to 2.5
Outputs:
- grad_features: float32 [9, 1, 128, 128, 128], P(None, None, 'row', 'col')
- grad_w_in: float32 [9, 256], replicated
- grad_b_in: float32 [256], replicated
- grad_w_mid: float32 [256, 256], replicated
- grad_b_mid: float32 [256], replicated
- grad_w_out: float32 [256, 6], replicated
The draws below stay inside these ranges and needn't reach their ends.
All inputs are finite; a program needn't handle non-finite values.
Results may differ from the reference program's by a relative error of at most 0.025.
Values sent between devices are 32-bit elements; how exact they have to be, the bound alone decides.
A program may use at most 128 MiB of HBM per device.

```python
import math
import jax
import jax.numpy as jnp
from jax import lax

NX = 128
NY = 128
NZ = 128
FEAT = 9
HID = 256
OUT = 6
SAMPLES = 1
CELLS = 2097152


def draw_features(key, part):
    shape = (FEAT, SAMPLES, NX, NY, NZ)
    base_key = jax.random.fold_in(key, 11)
    scale_key = jax.random.fold_in(key, 12)
    spread = jnp.exp(jax.random.uniform(scale_key, shape, jnp.float32, math.log(0.3), math.log(3.0)))
    base = jnp.clip(jax.random.normal(base_key, shape, jnp.float32), -4.0, 4.0)
    return (base * spread).astype(jnp.bfloat16)


def draw_cotangent(key, part):
    shape = (3, SAMPLES, NX, NY, NZ)
    base_key = jax.random.fold_in(key, 21)
    scale_key = jax.random.fold_in(key, 22)
    spread = jnp.exp(jax.random.uniform(scale_key, shape, jnp.float32, math.log(0.3), math.log(3.0)))
    base = jnp.clip(jax.random.normal(base_key, shape, jnp.float32), -4.0, 4.0) * spread
    return base.astype(jnp.float32)


def scatter_about(key, shape, width, most, held_as=jnp.bfloat16):
    result = width * jax.random.normal(key, shape, jnp.float32)
    return jnp.clip(result, min=-most, max=most).astype(held_as)


def setup_inputs(seed: int = 0) -> dict:
    key_of = jax.random.split(jax.random.key(seed), 8)
    features = draw_features(jax.random.fold_in(key_of[7], 71), 0)
    cotangent = draw_cotangent(jax.random.fold_in(key_of[7], 71), 0)
    w_in = scatter_about(key_of[2], (FEAT, HID), FEAT ** -0.5, 2.0)
    bias_in = scatter_about(key_of[3], (HID,), 0.5, 3.0, jnp.float32)
    w_mid = scatter_about(key_of[4], (HID, HID), HID ** -0.5, 0.375)
    bias_mid = scatter_about(key_of[5], (HID,), 0.5, 3.0, jnp.float32)
    w_out = scatter_about(key_of[6], (HID, OUT), OUT ** -0.5, 2.5)
    return dict(features=features, cotangent=cotangent, w_in=w_in, bias_in=bias_in, w_mid=w_mid, bias_mid=bias_mid, w_out=w_out)


STEP_DT = 0.04
PAIRS = ((0, 0), (1, 1), (2, 2), (0, 1), (0, 2), (1, 2))

def integer_modes(length):
    index = jnp.arange(length, dtype=jnp.int32)
    return jnp.where(index < length // 2, index, index - length)

def stress_adjoint(cotangent):
    spectra = jnp.fft.fftn(cotangent, axes=(2, 3, 4))
    modes_x = integer_modes(NX)[:, None, None]
    modes_y = integer_modes(NY)[None, :, None]
    modes_z = integer_modes(NZ)[None, None, :]
    keep = (3 * jnp.abs(modes_x) < NX) & (3 * jnp.abs(modes_y) < NY) & (3 * jnp.abs(modes_z) < NZ)
    waves = [modes_x.astype(jnp.float32), modes_y.astype(jnp.float32), modes_z.astype(jnp.float32)]
    inner = waves[0] * spectra[0] + waves[1] * spectra[1] + waves[2] * spectra[2]
    square = jnp.maximum(waves[0] * waves[0] + waves[1] * waves[1] + waves[2] * waves[2], 1.0)
    projected = [jnp.where(keep, spectra[comp] - waves[comp] * inner / square, 0.0) for comp in range(3)]
    pieces = []
    for first, second in PAIRS:
        if first == second:
            value = waves[first] * projected[first]
        else:
            value = waves[second] * projected[first] + waves[first] * projected[second]
        pieces.append(1j * STEP_DT * value)
    stress_hat = jnp.stack(pieces)
    return jnp.real(jnp.fft.ifftn(stress_hat, axes=(2, 3, 4))).astype(jnp.float32)

def closure_block(x_blk, g_blk, w_in, bias_in, w_mid, bias_mid, w_out):
    pre_in = jnp.dot(w_in.T, x_blk, preferred_element_type=jnp.float32) + bias_in[:, None]
    act_in = jnp.tanh(pre_in).astype(jnp.bfloat16)
    pre_mid = jnp.dot(w_mid.T, act_in, preferred_element_type=jnp.float32) + bias_mid[:, None]
    act_mid = jnp.tanh(pre_mid).astype(jnp.bfloat16)
    back_mid = jnp.dot(w_out, g_blk, preferred_element_type=jnp.float32)
    delta_mid = (back_mid * (1.0 - jnp.square(act_mid.astype(jnp.float32)))).astype(jnp.bfloat16)
    back_in = jnp.dot(w_mid, delta_mid, preferred_element_type=jnp.float32)
    delta_in = (back_in * (1.0 - jnp.square(act_in.astype(jnp.float32)))).astype(jnp.bfloat16)
    grad_x = jnp.dot(w_in, delta_in, preferred_element_type=jnp.float32)
    gw_out = jnp.dot(act_mid, g_blk.T, preferred_element_type=jnp.float32)
    gw_mid = jnp.dot(act_in, delta_mid.T, preferred_element_type=jnp.float32)
    gw_in = jnp.dot(x_blk, delta_in.T, preferred_element_type=jnp.float32)
    gb_mid = lax.optimization_barrier(jnp.sum(delta_mid.astype(jnp.float32), axis=1))
    gb_in = lax.optimization_barrier(jnp.sum(delta_in.astype(jnp.float32), axis=1))
    return (grad_x, (gw_in, gb_in, gw_mid, gb_mid, gw_out))

def reference(features, cotangent, w_in, bias_in, w_mid, bias_mid, w_out):
    stress = stress_adjoint(cotangent)
    grads = stress.astype(jnp.bfloat16).reshape(OUT, CELLS)
    feats = features.reshape(FEAT, CELLS)
    block = math.gcd(CELLS, 16384)
    count = CELLS // block

    def visit(carry, index):
        start = (index * block).astype(jnp.int32)
        x_blk = lax.dynamic_slice_in_dim(feats, start, block, 1)
        g_blk = lax.dynamic_slice_in_dim(grads, start, block, 1)
        grad_x, parts = closure_block(x_blk, g_blk, w_in, bias_in, w_mid, bias_mid, w_out)
        return (tuple((a + b for a, b in zip(carry, parts))), grad_x)
    init = (jnp.zeros((FEAT, HID), jnp.float32), jnp.zeros((HID,), jnp.float32), jnp.zeros((HID, HID), jnp.float32), jnp.zeros((HID,), jnp.float32), jnp.zeros((HID, OUT), jnp.float32))
    totals, pieces = lax.scan(visit, init, jnp.arange(count, dtype=jnp.int32))
    grad_features = jnp.moveaxis(pieces, 0, 1).reshape(FEAT, SAMPLES, NX, NY, NZ)
    factor = 1.0 / math.sqrt(CELLS)
    return (grad_features, totals[0] * factor, totals[1] * factor, totals[2] * factor, totals[3] * factor, totals[4] * factor)
```

```python
import functools
import math

import jax
import jax.numpy as jnp
import numpy as np
from jax import lax
from jax.experimental import pallas as pl
from jax.experimental.pallas import tpu as pltpu
from jax.sharding import PartitionSpec as P

STEP_DT = 0.04
MESH = pl.DeviceIdType.MESH


def kept_modes(length):
    top = (length - 1) // 3
    return top


def padded(values, parts):
    share = -(-len(values) // parts)
    out = np.zeros((parts * share,), np.int64)
    out[: len(values)] = values
    live = np.zeros((parts * share,), np.float64)
    live[: len(values)] = 1.0
    return out.reshape(parts, share), live.reshape(parts, share)


def angles(modes, length):
    pos = np.arange(length)
    turns = (modes[..., None] * pos) % length
    return turns * (2.0 * math.pi / length)


def f32(a):
    return jnp.asarray(np.ascontiguousarray(a), jnp.float32)


def bf16(a):
    return jnp.asarray(np.ascontiguousarray(a), jnp.bfloat16)


class Plan:
    def __init__(self, shape, rows, cols):
        self.nc, _, self.bx, self.by, self.nz = shape
        self.rows, self.cols = rows, cols
        self.nx, self.ny = self.bx * rows, self.by * cols
        self.mz, self.live_z = padded(np.arange(kept_modes(self.nz) + 1), cols)
        top_y, top_x = kept_modes(self.ny), kept_modes(self.nx)
        self.my, self.live_y = padded(np.arange(-top_y, top_y + 1), rows)
        self.mx = np.arange(-top_x, top_x + 1)
        self.kz, self.ky, self.kx = self.mz.shape[1], self.my.shape[1], len(self.mx)
        self.kxp = 8 * (-(-self.kx // 8))
        self.xl = max(d for d in range(1, self.bx + 1) if self.bx % d == 0 and d * self.by <= 128)
        self.xg = self.bx // self.xl
        self.wide = self.xl * self.by
        self.group = self.nc * self.xg
        self.gp = self.group
        while (2 * self.kz * self.gp) % 8 or (self.kz * self.gp * self.xl) % 8:
            self.gp += 1
        self.modes = 8 * (-(-2 * self.kz // 8))
        self.rows1 = 2 * self.kz * self.gp
        self.rows2 = self.nc * 2 * self.bx
        self.nf = 4
        self.rows3 = self.nf * 2 * self.bx
        self.ns = 5
        self.sx = self.ns * self.xg
        self.rows4 = 8 * (-(-2 * self.kz * self.sx // 8))

    def tables(self):
        kz, ky, kx, kxp = self.kz, self.ky, self.kx, self.kxp
        rows, cols, bx, by = self.rows, self.cols, self.bx, self.by
        az = angles(self.mz, self.nz)
        lz = self.live_z[..., None]
        t1 = np.zeros((cols, self.modes, self.nz))
        t1[:, :kz] = np.cos(az) * lz
        t1[:, kz : 2 * kz] = -np.sin(az) * lz
        weight = np.where(self.mz == 0, 1.0, 2.0)[..., None] * lz / self.nz
        t6 = np.zeros((cols, self.modes, self.nz))
        t6[:, :kz] = np.cos(az) * weight
        t6[:, kz : 2 * kz] = -np.sin(az) * weight
        ay = angles(self.my, self.ny)
        cy = np.cos(ay) * self.live_y[..., None]
        sy = np.sin(ay) * self.live_y[..., None]
        t2 = np.zeros((rows, 2, self.ny, 2, 128))
        t5 = np.zeros((rows, 2, 128, 2, self.ny))
        for k in range(ky):
            at = k * kz
            t2[:, 0, :, 0, at] = cy[:, k]
            t2[:, 1, :, 0, at] = sy[:, k]
            t2[:, 0, :, 1, at] = -sy[:, k]
            t2[:, 1, :, 1, at] = cy[:, k]
            t5[:, 0, at, 0] = cy[:, k] / self.ny
            t5[:, 1, at, 0] = -sy[:, k] / self.ny
            t5[:, 0, at, 1] = sy[:, k] / self.ny
            t5[:, 1, at, 1] = cy[:, k] / self.ny
        ax = angles(self.mx, self.nx)
        cx, sx = np.cos(ax), np.sin(ax)
        t3 = np.zeros((2, kxp, rows, 2, bx))
        t4 = np.zeros((rows, 2, bx, 2, kxp))
        cr, sr = cx.reshape(kx, rows, bx), sx.reshape(kx, rows, bx)
        t3[0, :kx, :, 0] = cr
        t3[0, :kx, :, 1] = sr
        t3[1, :kx, :, 0] = -sr
        t3[1, :kx, :, 1] = cr
        scale = STEP_DT / self.nx
        ci, si = cr.transpose(1, 2, 0) * scale, sr.transpose(1, 2, 0) * scale
        t4[:, 0, :, 0, :kx] = -si
        t4[:, 0, :, 1, :kx] = -ci
        t4[:, 1, :, 0, :kx] = ci
        t4[:, 1, :, 1, :kx] = -si
        lane_y = np.zeros((rows, 1, 128))
        lane_z = np.zeros((cols, 1, 128))
        lane_y[:, 0, : ky * kz] = np.repeat(self.my, kz, axis=1)
        lane_z[:, 0, : ky * kz] = np.tile(self.mz, (1, ky))
        wave_x = np.zeros((kxp, 128))
        wave_x[:kx] = self.mx[:, None]
        return (
            bf16(t1.reshape(cols * self.modes, self.nz)),
            bf16(t2.reshape(rows, 2 * self.ny, 256)),
            bf16(t3.reshape(2 * kxp, rows * 2 * bx)),
            bf16(t4.reshape(rows * 2 * bx, 2 * kxp)),
            bf16(t5.reshape(rows * 256, 2 * self.ny)),
            bf16(t6.reshape(cols * self.modes, self.nz)),
            f32(wave_x),
            f32(lane_y),
            f32(lane_z),
        )


def spectral_kernel(p, cot, t1, t2, t3, t4, t5, t6, wx_ref, wy_ref, wz_ref, out,
                    s1, d1, s2, d2, s3, d3, s4, d4, e2, q5, o5,
                    send1, recv1, send2, recv2, send3, recv3, send4, recv4):
    me_r, me_c = lax.axis_index("row"), lax.axis_index("col")
    rows, cols, kz, ky, kxp = p.rows, p.cols, p.kz, p.ky, p.kxp
    bx, by, nc = p.bx, p.by, p.nc
    last = (((1,), (1,)), ((), ()))
    first = (((0,), (0,)), ((), ()))
    half = jnp.bfloat16

    def row_peer(d):
        return lax.rem(me_r + d, rows)

    def col_peer(d):
        return lax.rem(me_c + d, cols)

    barrier = pltpu.get_barrier_semaphore()
    for d in range(1, rows):
        pl.semaphore_signal(barrier, inc=1, device_id=(row_peer(d), me_c), device_id_type=MESH)
    for d in range(1, cols):
        pl.semaphore_signal(barrier, inc=1, device_id=(me_r, col_peer(d)), device_id_type=MESH)

    def over_col(src, dst, send, recv):
        copies = []
        for d in range(1, cols):
            copy = pltpu.make_async_remote_copy(
                src_ref=src.at[col_peer(d)], dst_ref=dst.at[me_c], send_sem=send.at[d],
                recv_sem=recv.at[d], device_id=(me_r, col_peer(d)), device_id_type=MESH,
            )
            copy.start()
            copies.append(copy)
        dst[me_c] = src[me_c]
        return copies

    def over_row(src, dst, send, recv):
        copies = []
        for d in range(1, rows):
            copy = pltpu.make_async_remote_copy(
                src_ref=src.at[row_peer(d)], dst_ref=dst.at[me_r], send_sem=send.at[d],
                recv_sem=recv.at[d], device_id=(row_peer(d), me_c), device_id_type=MESH,
            )
            copy.start()
            copies.append(copy)
        dst[me_r] = src[me_r]
        return copies

    if p.gp > p.group or p.wide < 128:
        s1[...] = jnp.zeros_like(s1)
    for g in range(p.group):
        a = cot[pl.ds(g * p.wide, p.wide), :].astype(half)
        part = lax.dot_general(t1[...], a, last, preferred_element_type=jnp.float32)
        for c in range(cols):
            s1[c, pl.ds(g, 2 * kz, stride=p.gp), pl.ds(0, p.wide)] = part[
                c * p.modes : c * p.modes + 2 * kz
            ]
    pl.semaphore_wait(barrier, rows + cols - 2)
    moves1 = over_col(s1, d1, send1, recv1)
    for copy in moves1:
        copy.wait_recv()
    count = kz * p.gp
    where = lax.broadcasted_iota(jnp.int32, (count, 128), 1) // by
    for ri in range(2):
        for j in range(p.xl):
            whole = None
            for c in range(cols):
                tile = d1[c, pl.ds(ri * count, count), :]
                shift = ((c - j) * by) % 128
                tile = tile if shift == 0 else pltpu.roll(tile, shift, 1)
                whole = tile if whole is None else jnp.where(where == c, tile, whole)
            e2[ri, pl.ds(j, count, stride=p.xl), :] = whole
    lhs = jnp.concatenate([e2[0].astype(half), e2[1].astype(half)], axis=1)
    per = p.gp * p.xl
    for r in range(rows):
        part = jnp.dot(lhs, t2[r], preferred_element_type=jnp.float32)
        for ri in range(2):
            total = part[:per, ri * 128 : (ri + 1) * 128]
            for k in range(1, kz):
                total = total + pltpu.roll(
                    part[k * per : (k + 1) * per, ri * 128 : (ri + 1) * 128], k, 1
                )
            for v in range(nc):
                s2[r, pl.ds((2 * v + ri) * bx, bx), :] = total[v * bx : (v + 1) * bx]
    moves2 = over_row(s2, d2, send2, recv2)
    wx = wx_ref[...]
    wy, wz = wy_ref[me_r], wz_ref[me_c]
    for copy in moves2:
        copy.wait_recv()
    vel = []
    for v in range(nc):
        data = jnp.concatenate([d2[r, pl.ds(2 * v * bx, 2 * bx), :] for r in range(rows)], axis=0)
        hat = jnp.dot(t3[...], data.astype(half), preferred_element_type=jnp.float32)
        vel.append((hat[:kxp], hat[kxp:]))
    inverse = 1.0 / jnp.maximum(wx * wx + wy * wy + wz * wz, 1.0)
    fields = [[], [], [], []]
    for ri in range(2):
        inner = (wx * vel[0][ri] + wy * vel[1][ri] + wz * vel[2][ri]) * inverse
        px = vel[0][ri] - wx * inner
        py = vel[1][ri] - wy * inner
        pz = vel[2][ri] - wz * inner
        fields[0].append(py)
        fields[1].append(pz)
        fields[2].append(wy * px + wx * py)
        fields[3].append(wz * px + wx * pz)
    for f in range(p.nf):
        data = jnp.concatenate(fields[f], axis=0).astype(half)
        part = jnp.dot(t4[...], data, preferred_element_type=jnp.float32)
        for r in range(rows):
            s3[r, pl.ds(f * 2 * bx, 2 * bx), :] = part[r * 2 * bx : (r + 1) * 2 * bx]
    moves3 = over_row(s3, d3, send3, recv3)
    for copy in moves3:
        copy.wait_recv()
    span = p.ns * bx
    for r in range(rows):
        wy = wy_ref[r]
        for ri in range(2):
            qy, qz, xy, xz = [d3[r, pl.ds((2 * f + ri) * bx, bx), :] for f in range(p.nf)]
            data = jnp.concatenate([wy * qy, wz * qz, xy, xz, wz * qy + wy * qz], axis=0)
            for k in range(kz):
                tile = data if k == 0 else pltpu.roll(data, 128 - k, 1)
                q5[pl.ds(k * span, span), pl.ds((2 * r + ri) * 128, 128)] = tile
    part = jnp.dot(q5[...].astype(half), t5[...], preferred_element_type=jnp.float32)
    for ri in range(2):
        o5[ri] = part[:, ri * 128 : (ri + 1) * 128]
    count = kz * p.sx
    where = lax.broadcasted_iota(jnp.int32, (count, 128), 1) // by
    for ri in range(2):
        tiles = [o5[ri, pl.ds(j, count, stride=p.xl), :] for j in range(p.xl)]
        for c in range(cols):
            whole = None
            for j in range(p.xl):
                shift = ((j - c) * by) % 128
                tile = tiles[j] if shift == 0 else pltpu.roll(tiles[j], shift, 1)
                whole = tile if whole is None else jnp.where(where == j, tile, whole)
            s4[c, pl.ds(ri * count, count), :] = whole
    moves4 = over_col(s4, d4, send4, recv4)
    for copy in moves4:
        copy.wait_recv()
    pad = jnp.zeros((p.modes - 2 * kz, 128), jnp.float32)
    for g in range(p.xg):
        comps = []
        for comp in range(p.ns):
            pieces = []
            for c in range(cols):
                pieces.append(d4[c, pl.ds(comp * p.xg + g, 2 * kz, stride=p.sx), :])
                if p.modes > 2 * kz:
                    pieces.append(pad)
            data = jnp.concatenate(pieces, axis=0).astype(half)
            comps.append(
                lax.dot_general(data, t6[...], first, preferred_element_type=jnp.float32)[: p.wide]
            )
        order = [-(comps[0] + comps[1]), comps[0], comps[1], comps[2], comps[3], comps[4]]
        for comp in range(6):
            out[comp, pl.ds(g * p.wide, p.wide), :] = order[comp].astype(out.dtype)
    for copy in moves1 + moves2 + moves3 + moves4:
        copy.wait_send()


def spectral(cotangent, rows, cols):
    p = Plan(cotangent.shape, rows, cols)
    dma = pltpu.SemaphoreType.DMA
    vmem = pl.BlockSpec(memory_space=pltpu.VMEM)
    single = jnp.float32
    return pl.pallas_call(
        functools.partial(spectral_kernel, p),
        out_shape=jax.ShapeDtypeStruct((6, p.bx * p.by, p.nz), jnp.bfloat16),
        in_specs=[vmem] * 10,
        out_specs=vmem,
        scratch_shapes=[
            pltpu.VMEM((cols, p.rows1, 128), single), pltpu.VMEM((cols, p.rows1, 128), single),
            pltpu.VMEM((rows, p.rows2, 128), single), pltpu.VMEM((rows, p.rows2, 128), single),
            pltpu.VMEM((rows, p.rows3, 128), single), pltpu.VMEM((rows, p.rows3, 128), single),
            pltpu.VMEM((cols, p.rows4, 128), single), pltpu.VMEM((cols, p.rows4, 128), single),
            pltpu.VMEM((2, p.kz * p.gp * p.xl, 128), single),
            pltpu.VMEM((p.kz * p.ns * p.bx, rows * 256), single),
            pltpu.VMEM((2, p.kz * p.ns * p.bx, 128), single),
            dma((cols,)), dma((cols,)), dma((rows,)), dma((rows,)),
            dma((rows,)), dma((rows,)), dma((cols,)), dma((cols,)),
        ],
        compiler_params=pltpu.CompilerParams(
            collective_id=1, has_side_effects=True, vmem_limit_bytes=48 << 20
        ),
        name="spectral",
    )(cotangent.reshape(p.nc * p.bx * p.by, p.nz), *p.tables())


def closure_kernel(steps, feat, s_ref, w1_ref, b1_ref, w2t_ref, w2_ref, b2_ref, wo_ref, wi_ref,
                   gx_ref, out_ref, accm, acci, acco, accb):
    step = pl.program_id(0)
    hid = w2_ref.shape[0]
    ext = s_ref.shape[0]
    first = (((0,), (0,)), ((), ()))
    last = (((1,), (1,)), ((), ()))

    @pl.when(step == 0)
    def _():
        accm[...] = jnp.zeros_like(accm)
        acci[...] = jnp.zeros_like(acci)
        acco[...] = jnp.zeros_like(acco)
        accb[...] = jnp.zeros_like(accb)

    s = s_ref[...]
    pre = lax.dot_general(s, w1_ref[...], first, preferred_element_type=jnp.float32) + b1_ref[...]
    act_in = jnp.tanh(pre).astype(jnp.bfloat16)
    pre = jnp.dot(act_in, w2_ref[...], preferred_element_type=jnp.float32) + b2_ref[...]
    act_mid = jnp.tanh(pre).astype(jnp.bfloat16)
    wide = act_mid.astype(jnp.float32)
    back = lax.dot_general(s, wo_ref[...], first, preferred_element_type=jnp.float32)
    delta_mid = (back * (1.0 - wide * wide)).astype(jnp.bfloat16)
    accb[...] += jnp.sum(delta_mid.astype(jnp.float32), axis=0, keepdims=True)
    acco[...] += jnp.dot(s, act_mid, preferred_element_type=jnp.float32)
    accm[...] += lax.dot_general(act_in, delta_mid, first, preferred_element_type=jnp.float32)
    back = jnp.dot(delta_mid, w2t_ref[...], preferred_element_type=jnp.float32)
    wide = act_in.astype(jnp.float32)
    delta_in = (back * (1.0 - wide * wide)).astype(jnp.bfloat16)
    acci[...] += jnp.dot(s, delta_in, preferred_element_type=jnp.float32)
    grad = lax.dot_general(wi_ref[...], delta_in, last, preferred_element_type=jnp.float32)
    for row in range(gx_ref.shape[1]):
        gx_ref[:, row, :] = grad[:feat, row * 128 : (row + 1) * 128]

    @pl.when(step == steps - 1)
    def _():
        out_ref[...] = jnp.zeros_like(out_ref)
        out_ref[pl.ds(0, hid), :] = accm[...]
        out_ref[pl.ds(hid, ext), :] = acci[...]
        row = lax.broadcasted_iota(jnp.int32, (ext, hid), 0)
        out_ref[pl.ds(hid + ext, ext), :] = jnp.where(row == feat, accb[...], acco[...])


def closure(sources, feat, w_in, bias_in, w_mid, bias_mid, w_out, out_rows):
    ext, cells = sources.shape
    hid = w_mid.shape[0]
    block = math.gcd(cells, 4096)
    steps = cells // block
    outs = w_out.shape[1]
    wi = jnp.concatenate([w_in, jnp.zeros((ext - feat, hid), jnp.bfloat16)], axis=0)
    wo = jnp.concatenate([jnp.zeros((ext - outs, hid), jnp.bfloat16), w_out.T], axis=0)
    whole = lambda shape: pl.BlockSpec(shape, lambda i: (0, 0))
    return pl.pallas_call(
        functools.partial(closure_kernel, steps, feat),
        grid=(steps,),
        in_specs=[
            pl.BlockSpec((ext, block), lambda i: (0, i)),
            whole((ext, hid)),
            whole((1, hid)),
            whole((hid, hid)),
            whole((hid, hid)),
            whole((1, hid)),
            whole((ext, hid)),
            whole((ext, hid)),
        ],
        out_specs=[
            pl.BlockSpec((feat, block // 128, 128), lambda i: (0, i, 0)),
            whole((out_rows, hid)),
        ],
        out_shape=[
            jax.ShapeDtypeStruct((feat, cells // 128, 128), jnp.float32),
            jax.ShapeDtypeStruct((out_rows, hid), jnp.float32),
        ],
        scratch_shapes=[
            pltpu.VMEM((hid, hid), jnp.float32),
            pltpu.VMEM((ext, hid), jnp.float32),
            pltpu.VMEM((ext, hid), jnp.float32),
            pltpu.VMEM((1, hid), jnp.float32),
        ],
        compiler_params=pltpu.CompilerParams(vmem_limit_bytes=48 << 20),
        name="closure",
    )(sources, wi, bias_in[None], w_mid.T, w_mid, bias_mid[None], wo, wi)


def reduce_kernel(rows, cols, factor, g_ref, o_ref, rbuf, cbuf, send_r, recv_r, send_c, recv_c,
                  send_o, recv_o):
    me_r, me_c = lax.axis_index("row"), lax.axis_index("col")
    barrier = pltpu.get_barrier_semaphore()
    for d in range(1, rows):
        pl.semaphore_signal(
            barrier, inc=1, device_id=(lax.rem(me_r + d, rows), me_c), device_id_type=MESH
        )
    for d in range(1, cols):
        pl.semaphore_signal(
            barrier, inc=1, device_id=(me_r, lax.rem(me_c + d, cols)), device_id_type=MESH
        )
    pl.semaphore_wait(barrier, rows + cols - 2)
    first = []
    for d in range(1, rows):
        peer = lax.rem(me_r + d, rows)
        copy = pltpu.make_async_remote_copy(
            src_ref=g_ref.at[peer], dst_ref=rbuf.at[d], send_sem=send_r.at[d],
            recv_sem=recv_r.at[d], device_id=(peer, me_c), device_id_type=MESH,
        )
        copy.start()
        first.append(copy)
    total = g_ref[me_r]
    for d in range(1, rows):
        first[d - 1].wait_recv()
        total = total + rbuf[d]
    cbuf[me_c] = total
    second = []
    for d in range(1, cols):
        copy = pltpu.make_async_remote_copy(
            src_ref=cbuf.at[me_c], dst_ref=cbuf.at[me_c], send_sem=send_c.at[d],
            recv_sem=recv_c.at[d], device_id=(me_r, lax.rem(me_c + d, cols)), device_id_type=MESH,
        )
        copy.start()
        second.append(copy)
    for copy in second:
        copy.wait_recv()
    total = cbuf[0]
    for c in range(1, cols):
        total = total + cbuf[c]
    o_ref[me_r] = total * factor
    third = []
    for d in range(1, rows):
        copy = pltpu.make_async_remote_copy(
            src_ref=o_ref.at[me_r], dst_ref=o_ref.at[me_r], send_sem=send_o.at[d],
            recv_sem=recv_o.at[d], device_id=(lax.rem(me_r + d, rows), me_c), device_id_type=MESH,
        )
        copy.start()
        third.append(copy)
    for copy in third:
        copy.wait_recv()
    for copy in first + second + third:
        copy.wait_send()


def reduce_all(grads, rows, cols, factor):
    _, share, width = grads.shape
    dma = pltpu.SemaphoreType.DMA
    return pl.pallas_call(
        functools.partial(reduce_kernel, rows, cols, factor),
        out_shape=jax.ShapeDtypeStruct(grads.shape, jnp.float32),
        in_specs=[pl.BlockSpec(memory_space=pltpu.VMEM)],
        out_specs=pl.BlockSpec(memory_space=pltpu.VMEM),
        scratch_shapes=[
            pltpu.VMEM((rows, share, width), jnp.float32),
            pltpu.VMEM((cols, share, width), jnp.float32),
            dma((rows,)), dma((rows,)), dma((cols,)), dma((cols,)), dma((rows,)), dma((rows,)),
        ],
        compiler_params=pltpu.CompilerParams(collective_id=0, has_side_effects=True),
        name="reduce_all",
    )(grads)


def per_device(features, cotangent, w_in, bias_in, w_mid, bias_mid, w_out, rows, cols):
    stress = spectral(cotangent, rows, cols)
    feat, outs = features.shape[0], w_out.shape[1]
    hid = w_mid.shape[0]
    cells = math.prod(features.shape[1:])
    ext = 16 * (-(-(feat + 1 + outs) // 16))
    sources = jnp.concatenate(
        [
            features.reshape(feat, cells),
            jnp.ones((ext - feat - outs, cells), jnp.bfloat16),
            stress.reshape(outs, cells),
        ],
        axis=0,
    )
    share = 8 * (-(-(hid + 2 * ext) // (8 * rows)))
    field, grads = closure(
        sources, feat, w_in, bias_in, w_mid, bias_mid, w_out, rows * share
    )
    factor = 1.0 / math.sqrt(cells * rows * cols)
    total = reduce_all(grads.reshape(rows, share, hid), rows, cols, factor)
    total = total.reshape(rows * share, hid)
    last = hid + ext
    return (
        field.reshape(features.shape),
        total[hid : hid + feat],
        total[hid + feat],
        total[:hid],
        total[last + feat],
        total[last + ext - outs : last + ext].T,
    )


def solution(mesh):
    body = functools.partial(per_device, rows=mesh.shape["row"], cols=mesh.shape["col"])
    return jax.shard_map(
        body,
        mesh=mesh,
        in_specs=(
            P(None, None, "row", "col", None),
            P(None, None, "row", "col", None),
            P(),
            P(),
            P(),
            P(),
            P(),
        ),
        out_specs=(P(None, None, "row", "col", None), P(), P(), P(), P(), P()),
        check_vma=False,
    )
```

```python
import functools
import math

import jax
import jax.numpy as jnp
import numpy as np
from jax import lax
from jax.experimental import pallas as pl
from jax.experimental.pallas import tpu as pltpu
from jax.sharding import PartitionSpec as P

STEP_DT = 0.04
MESH = pl.DeviceIdType.MESH


def kept_modes(length):
    top = (length - 1) // 3
    return top


def padded(values, parts):
    share = -(-len(values) // parts)
    out = np.zeros((parts * share,), np.int64)
    out[: len(values)] = values
    live = np.zeros((parts * share,), np.float64)
    live[: len(values)] = 1.0
    return out.reshape(parts, share), live.reshape(parts, share)


def angles(modes, length):
    pos = np.arange(length)
    turns = (modes[..., None] * pos) % length
    return turns * (2.0 * math.pi / length)


def f32(a):
    return jnp.asarray(np.ascontiguousarray(a), jnp.float32)


def bf16(a):
    return jnp.asarray(np.ascontiguousarray(a), jnp.bfloat16)


def up(value, step):
    return step * (-(-value // step))


class Plan:
    def __init__(self, shape, rows, cols):
        self.nc, _, self.bx, self.by, self.nz = shape
        self.rows, self.cols = rows, cols
        self.nx, self.ny = self.bx * rows, self.by * cols
        self.mz, self.live_z = padded(np.arange(kept_modes(self.nz) + 1), cols)
        top_y, top_x = kept_modes(self.ny), kept_modes(self.nx)
        self.my, self.live_y = padded(np.arange(-top_y, top_y + 1), rows)
        self.mx = np.arange(-top_x, top_x + 1)
        self.kz, self.ky, self.kx = self.mz.shape[1], self.my.shape[1], len(self.mx)
        self.kxp = 8 * (-(-self.kx // 8))
        self.xl = max(d for d in range(1, self.bx + 1) if self.bx % d == 0 and d * self.by <= 128)
        self.xg = self.bx // self.xl
        self.wide = self.xl * self.by
        self.parts = 2 if self.xg % 2 == 0 and (self.bx // 2) % 8 == 0 else 1
        self.hg, self.hx = self.xg // self.parts, self.bx // self.parts
        self.gp = self.nc * self.hg
        while (self.kz * self.gp * self.xl) % 8:
            self.gp += 1
        self.modes = up(2 * self.kz, 8)
        self.rows1 = up(2 * self.kz * self.gp, 8)
        self.rows2 = self.nc * 2 * self.hx
        self.nf, self.ns = 4, 5
        self.rows3 = self.nf * 2 * self.hx
        self.sx = self.ns * self.hg
        self.rows4 = up(2 * self.kz * self.sx, 8)
        self.lines = self.bx * self.by

    def tables(self):
        kz, ky, kx, kxp = self.kz, self.ky, self.kx, self.kxp
        rows, cols, bx, by = self.rows, self.cols, self.bx, self.by
        az = angles(self.mz, self.nz)
        lz = self.live_z[..., None]
        t1 = np.zeros((cols, self.modes, self.nz))
        t1[:, :kz] = np.cos(az) * lz
        t1[:, kz : 2 * kz] = -np.sin(az) * lz
        weight = np.where(self.mz == 0, 1.0, 2.0)[..., None] * lz / self.nz
        t6 = np.zeros((cols, self.modes, self.nz))
        t6[:, :kz] = np.cos(az) * weight
        t6[:, kz : 2 * kz] = -np.sin(az) * weight
        ay = angles(self.my, self.ny)
        cy = np.cos(ay) * self.live_y[..., None]
        sy = np.sin(ay) * self.live_y[..., None]
        t2 = np.zeros((rows, 2, self.ny, 2, 128))
        t5 = np.zeros((rows, 2, 128, 2, self.ny))
        for k in range(ky):
            at = k * kz
            t2[:, 0, :, 0, at] = cy[:, k]
            t2[:, 1, :, 0, at] = sy[:, k]
            t2[:, 0, :, 1, at] = -sy[:, k]
            t2[:, 1, :, 1, at] = cy[:, k]
            t5[:, 0, at, 0] = cy[:, k] / self.ny
            t5[:, 1, at, 0] = -sy[:, k] / self.ny
            t5[:, 0, at, 1] = sy[:, k] / self.ny
            t5[:, 1, at, 1] = cy[:, k] / self.ny
        ax = angles(self.mx, self.nx)
        cx, sx = np.cos(ax), np.sin(ax)
        parts, hx = self.parts, self.hx
        t3 = np.zeros((2, kxp, rows, 2, bx))
        t4 = np.zeros((rows, 2, bx, 2, kxp))
        cr, sr = cx.reshape(kx, rows, bx), sx.reshape(kx, rows, bx)
        t3[0, :kx, :, 0] = cr
        t3[0, :kx, :, 1] = sr
        t3[1, :kx, :, 0] = -sr
        t3[1, :kx, :, 1] = cr
        scale = STEP_DT / self.nx
        ci, si = cr.transpose(1, 2, 0) * scale, sr.transpose(1, 2, 0) * scale
        t4[:, 0, :, 0, :kx] = -si
        t4[:, 0, :, 1, :kx] = -ci
        t4[:, 1, :, 0, :kx] = ci
        t4[:, 1, :, 1, :kx] = -si
        t3 = t3.reshape(2, kxp, rows, 2, parts, hx).transpose(0, 1, 4, 2, 3, 5)
        t4 = t4.reshape(rows, 2, parts, hx, 2, kxp).transpose(2, 0, 1, 3, 4, 5)
        lane_y = np.zeros((rows, 1, 128))
        lane_z = np.zeros((cols, 1, 128))
        lane_y[:, 0, : ky * kz] = np.repeat(self.my, kz, axis=1)
        lane_z[:, 0, : ky * kz] = np.tile(self.mz, (1, ky))
        wave_x = np.zeros((kxp, 128))
        wave_x[:kx] = self.mx[:, None]
        return (
            bf16(t1.reshape(cols * self.modes, self.nz)),
            bf16(t2.reshape(rows, 2 * self.ny, 256)),
            bf16(t3.reshape(2 * kxp, rows * 2 * bx)),
            bf16(t4.reshape(parts, rows * 2 * hx, 2 * kxp)),
            bf16(t5.reshape(rows * 256, 2 * self.ny)),
            bf16(t6.reshape(cols * self.modes, self.nz)),
            f32(wave_x),
            f32(lane_y),
            f32(lane_z),
        )


def spectral_kernel(p, fp, cot, feat, w1_ref, b1_ref, w2_ref, b2_ref,
                    t1, t2, t3, t4, t5, t6, wx_ref, wy_ref, wz_ref,
                    sf_out, sg_out, act_in, act_mid,
                    s1, d1, s2, d2, s3, d3, s4, d4, e2, q5, o5, flat, abuf, mbuf,
                    send1, recv1, send2, recv2, send3, recv3, send4, recv4, sem_a, sem_m):
    me_r, me_c = lax.axis_index("row"), lax.axis_index("col")
    rows, cols, kz, ky, kxp = p.rows, p.cols, p.kz, p.ky, p.kxp
    bx, by, nc, hx, parts = p.bx, p.by, p.nc, p.hx, p.parts
    last = (((1,), (1,)), ((), ()))
    first = (((0,), (0,)), ((), ()))
    half = jnp.bfloat16

    def row_peer(d):
        return lax.rem(me_r + d, rows)

    def col_peer(d):
        return lax.rem(me_c + d, cols)

    barrier = pltpu.get_barrier_semaphore()
    for d in range(1, rows):
        pl.semaphore_signal(barrier, inc=1, device_id=(row_peer(d), me_c), device_id_type=MESH)
    for d in range(1, cols):
        pl.semaphore_signal(barrier, inc=1, device_id=(me_r, col_peer(d)), device_id_type=MESH)
    sends = []

    def over_col(h, src, dst, send, recv):
        copies = []
        for d in range(1, cols):
            copy = pltpu.make_async_remote_copy(
                src_ref=src.at[h, col_peer(d)], dst_ref=dst.at[h, me_c], send_sem=send.at[h, d],
                recv_sem=recv.at[h, d], device_id=(me_r, col_peer(d)), device_id_type=MESH,
            )
            copy.start()
            copies.append(copy)
        dst[h, me_c] = src[h, me_c]
        sends.extend(copies)
        return copies

    def over_row(h, src, dst, send, recv):
        copies = []
        for d in range(1, rows):
            copy = pltpu.make_async_remote_copy(
                src_ref=src.at[h, row_peer(d)], dst_ref=dst.at[h, me_r], send_sem=send.at[h, d],
                recv_sem=recv.at[h, d], device_id=(row_peer(d), me_c), device_id_type=MESH,
            )
            copy.start()
            copies.append(copy)
        dst[h, me_r] = src[h, me_r]
        sends.extend(copies)
        return copies

    def arrived(copies):
        for copy in copies:
            copy.wait_recv()

    steps, _, block = act_in.shape
    done = [0]

    def keep(i, slot):
        return (
            pltpu.make_async_copy(abuf.at[slot], act_in.at[i], sem_a.at[slot]),
            pltpu.make_async_copy(mbuf.at[slot], act_mid.at[i], sem_m.at[slot]),
        )

    def forward_block(i, carry):
        slot = lax.rem(i, 2)

        @pl.when(i >= 2)
        def _():
            for copy in keep(i, slot):
                copy.wait()

        src = sf_out[:, pl.ds(pl.multiple_of(i * block, block), block)]
        pre = jnp.dot(w1_ref[...], src, preferred_element_type=jnp.float32) + b1_ref[...]
        act = jnp.tanh(pre).astype(half)
        abuf[slot] = act
        pre = jnp.dot(w2_ref[...], act, preferred_element_type=jnp.float32) + b2_ref[...]
        mbuf[slot] = jnp.tanh(pre).astype(half)
        for copy in keep(i, slot):
            copy.start()
        return carry

    def forward(share):
        upto = min(steps, -(-steps * share // 16))
        if upto > done[0]:
            lax.fori_loop(done[0], upto, forward_block, 0)
            done[0] = upto

    def stage1(h):
        for v in range(nc):
            for g in range(p.hg):
                at = v * p.xg + h * p.hg + g
                a = cot[pl.ds(at * p.wide, p.wide), :].astype(half)
                part = lax.dot_general(t1[...], a, last, preferred_element_type=jnp.float32)
                for c in range(cols):
                    s1[h, c, pl.ds(v * p.hg + g, 2 * kz, stride=p.gp), pl.ds(0, p.wide)] = part[
                        c * p.modes : c * p.modes + 2 * kz
                    ]

    def stage2(h):
        count = kz * p.gp
        where = lax.broadcasted_iota(jnp.int32, (count, 128), 1) // by
        for ri in range(2):
            for j in range(p.xl):
                whole = None
                for c in range(cols):
                    tile = d1[h, c, pl.ds(ri * count, count), :]
                    shift = ((c - j) * by) % 128
                    tile = tile if shift == 0 else pltpu.roll(tile, shift, 1)
                    whole = tile if whole is None else jnp.where(where == c, tile, whole)
                e2[ri, pl.ds(j, count, stride=p.xl), :] = whole
        lhs = jnp.concatenate([e2[0].astype(half), e2[1].astype(half)], axis=1)
        per = p.gp * p.xl
        for r in range(rows):
            part = jnp.dot(lhs, t2[r], preferred_element_type=jnp.float32)
            for ri in range(2):
                total = part[:per, ri * 128 : (ri + 1) * 128]
                for k in range(1, kz):
                    total = total + pltpu.roll(
                        part[k * per : (k + 1) * per, ri * 128 : (ri + 1) * 128], k, 1
                    )
                for v in range(nc):
                    s2[h, r, pl.ds((2 * v + ri) * hx, hx), :] = total[v * hx : (v + 1) * hx]

    def stage3():
        wx, wy, wz = wx_ref[...], wy_ref[me_r], wz_ref[me_c]
        vel = []
        for v in range(nc):
            data = jnp.concatenate(
                [d2[h, r, pl.ds(2 * v * hx, 2 * hx), :] for h in range(parts) for r in range(rows)],
                axis=0,
            )
            hat = jnp.dot(t3[...], data.astype(half), preferred_element_type=jnp.float32)
            vel.append((hat[:kxp], hat[kxp:]))
        inverse = 1.0 / jnp.maximum(wx * wx + wy * wy + wz * wz, 1.0)
        fields = [[], [], [], []]
        for ri in range(2):
            inner = (wx * vel[0][ri] + wy * vel[1][ri] + wz * vel[2][ri]) * inverse
            px = vel[0][ri] - wx * inner
            py = vel[1][ri] - wy * inner
            pz = vel[2][ri] - wz * inner
            fields[0].append(py)
            fields[1].append(pz)
            fields[2].append(wy * px + wx * py)
            fields[3].append(wz * px + wx * pz)
        return [jnp.concatenate(field, axis=0).astype(half) for field in fields]

    def stage4(h, fields):
        for f in range(p.nf):
            part = jnp.dot(t4[h], fields[f], preferred_element_type=jnp.float32)
            for r in range(rows):
                s3[h, r, pl.ds(f * 2 * hx, 2 * hx), :] = part[r * 2 * hx : (r + 1) * 2 * hx]

    def stage5(h):
        span = p.ns * hx
        for r in range(rows):
            wy, wz = wy_ref[r], wz_ref[me_c]
            for ri in range(2):
                qy, qz, xy, xz = [d3[h, r, pl.ds((2 * f + ri) * hx, hx), :] for f in range(p.nf)]
                data = jnp.concatenate([wy * qy, wz * qz, xy, xz, wz * qy + wy * qz], axis=0)
                for k in range(kz):
                    tile = data if k == 0 else pltpu.roll(data, 128 - k, 1)
                    q5[pl.ds(k * span, span), pl.ds((2 * r + ri) * 128, 128)] = tile
        part = jnp.dot(q5[...].astype(half), t5[...], preferred_element_type=jnp.float32)
        for ri in range(2):
            o5[ri] = part[:, ri * 128 : (ri + 1) * 128]
        count = kz * p.sx
        where = lax.broadcasted_iota(jnp.int32, (count, 128), 1) // by
        for ri in range(2):
            tiles = [o5[ri, pl.ds(j, count, stride=p.xl), :] for j in range(p.xl)]
            for c in range(cols):
                whole = None
                for j in range(p.xl):
                    shift = ((j - c) * by) % 128
                    tile = tiles[j] if shift == 0 else pltpu.roll(tiles[j], shift, 1)
                    whole = tile if whole is None else jnp.where(where == j, tile, whole)
                s4[h, c, pl.ds(ri * count, count), :] = whole

    def stage6(h):
        pad = jnp.zeros((p.modes - 2 * kz, 128), jnp.float32)
        for g in range(p.hg):
            comps = []
            for comp in range(p.ns):
                pieces = []
                for c in range(cols):
                    pieces.append(d4[h, c, pl.ds(comp * p.hg + g, 2 * kz, stride=p.sx), :])
                    if p.modes > 2 * kz:
                        pieces.append(pad)
                data = jnp.concatenate(pieces, axis=0).astype(half)
                comps.append(
                    lax.dot_general(data, t6[...], first, preferred_element_type=jnp.float32)[
                        : p.wide
                    ]
                )
            order = [-(comps[0] + comps[1]), comps[0], comps[1], comps[2], comps[3], comps[4]]
            line = (h * p.hg + g) * p.wide
            for comp in range(6):
                flat[pl.ds(line * 16 + comp, p.wide, stride=16), :] = order[comp]
            for n in range(p.wide):
                sg_out[:, pl.ds((line + n) * 128, 128)] = flat[
                    pl.ds((line + n) * 16, 16), :
                ].astype(half)

    def take_features():
        row = lax.broadcasted_iota(jnp.int32, (p.lines * 16, 128), 0)
        flat[...] = jnp.where(row % 16 == fp, 1.0, 0.0)
        for f in range(fp):
            flat[pl.ds(f, p.lines, stride=16), :] = feat[f].astype(jnp.float32)
        for n in range(p.lines):
            sf_out[:, pl.ds(n * 128, 128)] = flat[pl.ds(n * 16, 16), :].astype(half)
        flat[...] = jnp.zeros_like(flat)

    if p.wide < 128:
        s1[...] = jnp.zeros_like(s1)
    moves1, moves2, moves3, moves4 = [], [], [], []
    for h in range(parts):
        stage1(h)
        if h == 0:
            pl.semaphore_wait(barrier, rows + cols - 2)
        moves1.append(over_col(h, s1, d1, send1, recv1))
    take_features()
    forward(1)
    for h in range(parts):
        arrived(moves1[h])
        stage2(h)
        moves2.append(over_row(h, s2, d2, send2, recv2))
        forward(3 + 3 * h)
    for h in range(parts):
        arrived(moves2[h])
    fields = stage3()
    for h in range(parts):
        stage4(h, fields)
        moves3.append(over_row(h, s3, d3, send3, recv3))
    forward(10)
    for h in range(parts):
        arrived(moves3[h])
        stage5(h)
        moves4.append(over_col(h, s4, d4, send4, recv4))
        forward(13 + 3 * h)
    forward(16)
    for h in range(parts):
        arrived(moves4[h])
        stage6(h)
    for i in range(max(0, steps - 2), steps):
        for copy in keep(i, i % 2):
            copy.wait()
    for copy in sends:
        copy.wait_send()


def spectral(features, cotangent, w_in, bias_in, w_mid, bias_mid, rows, cols):
    p = Plan(cotangent.shape, rows, cols)
    feat, hid = w_in.shape
    cells = p.lines * p.nz
    block = math.gcd(cells, 4096)
    steps = cells // block
    dma = pltpu.SemaphoreType.DMA
    vmem = pl.BlockSpec(memory_space=pltpu.VMEM)
    hbm = pl.BlockSpec(memory_space=pl.ANY)
    single, half = jnp.float32, jnp.bfloat16
    w1 = jnp.concatenate([w_in.T, jnp.zeros((hid, 16 - feat), half)], axis=1)
    parts = p.parts
    return pl.pallas_call(
        functools.partial(spectral_kernel, p, feat),
        out_shape=[
            jax.ShapeDtypeStruct((16, cells), half),
            jax.ShapeDtypeStruct((16, cells), half),
            jax.ShapeDtypeStruct((steps, hid, block), half),
            jax.ShapeDtypeStruct((steps, hid, block), half),
        ],
        in_specs=[vmem] * 15,
        out_specs=[vmem, vmem, hbm, hbm],
        scratch_shapes=[
            pltpu.VMEM((parts, cols, p.rows1, 128), single),
            pltpu.VMEM((parts, cols, p.rows1, 128), single),
            pltpu.VMEM((parts, rows, p.rows2, 128), single),
            pltpu.VMEM((parts, rows, p.rows2, 128), single),
            pltpu.VMEM((parts, rows, p.rows3, 128), single),
            pltpu.VMEM((parts, rows, p.rows3, 128), single),
            pltpu.VMEM((parts, cols, p.rows4, 128), single),
            pltpu.VMEM((parts, cols, p.rows4, 128), single),
            pltpu.VMEM((2, p.kz * p.gp * p.xl, 128), single),
            pltpu.VMEM((p.kz * p.ns * p.hx, rows * 256), single),
            pltpu.VMEM((2, p.kz * p.ns * p.hx, 128), single),
            pltpu.VMEM((p.lines * 16, 128), single),
            pltpu.VMEM((2, hid, block), half),
            pltpu.VMEM((2, hid, block), half),
            dma((parts, cols)), dma((parts, cols)), dma((parts, rows)), dma((parts, rows)),
            dma((parts, rows)), dma((parts, rows)), dma((parts, cols)), dma((parts, cols)),
            dma((2,)), dma((2,)),
        ],
        compiler_params=pltpu.CompilerParams(
            collective_id=1, has_side_effects=True, vmem_limit_bytes=56 << 20
        ),
        name="spectral",
    )(
        cotangent.reshape(p.nc * p.lines, p.nz), features.reshape(feat, p.lines, p.nz),
        w1, bias_in[:, None], w_mid.T, bias_mid[:, None], *p.tables(),
    )


def closure_kernel(steps, feat, sf_ref, sg_ref, ai_ref, am_ref, w2_ref, wo_ref, wi_ref,
                   gx_ref, out_ref, cat, accm, acci, acco):
    step = pl.program_id(0)
    hid, block = ai_ref.shape[1:]
    half = jnp.bfloat16
    last = (((1,), (1,)), ((), ()))

    @pl.when(step == 0)
    def _():
        accm[...] = jnp.zeros_like(accm)
        acci[...] = jnp.zeros_like(acci)
        acco[...] = jnp.zeros_like(acco)

    sf, sg = sf_ref[...], sg_ref[...]
    act_mid = am_ref[0]
    cat[pl.ds(0, hid), :] = ai_ref[0]
    cat[pl.ds(hid, 16), :] = sf
    back = jnp.dot(wo_ref[...], sg, preferred_element_type=jnp.float32)
    wide = act_mid.astype(jnp.float32)
    delta_mid = (back * (1.0 - wide * wide)).astype(half)
    acco[...] += lax.dot_general(sg, act_mid, last, preferred_element_type=jnp.float32)
    accm[...] += lax.dot_general(cat[...], delta_mid, last, preferred_element_type=jnp.float32)
    back = jnp.dot(w2_ref[...], delta_mid, preferred_element_type=jnp.float32)
    wide = ai_ref[0].astype(jnp.float32)
    delta_in = (back * (1.0 - wide * wide)).astype(half)
    acci[...] += lax.dot_general(sf, delta_in, last, preferred_element_type=jnp.float32)
    grad = jnp.dot(wi_ref[...], delta_in, preferred_element_type=jnp.float32)
    for row in range(gx_ref.shape[1]):
        gx_ref[:, row, :] = grad[:feat, row * 128 : (row + 1) * 128]

    @pl.when(step == steps - 1)
    def _():
        out_ref[...] = jnp.zeros_like(out_ref)
        out_ref[pl.ds(0, hid + 16), :] = accm[...]
        out_ref[pl.ds(hid + 16, 16), :] = acci[...]
        out_ref[pl.ds(hid + 32, 16), :] = acco[...]


def closure(sf, sg, act_in, act_mid, w_in, w_mid, w_out, out_rows):
    steps, hid, block = act_in.shape
    feat, outs = w_in.shape[0], w_out.shape[1]
    cells = steps * block
    half = jnp.bfloat16
    wi = jnp.concatenate([w_in, jnp.zeros((16 - feat, hid), half)], axis=0)
    wo = jnp.concatenate([w_out, jnp.zeros((hid, 16 - outs), half)], axis=1)
    whole = lambda shape: pl.BlockSpec(shape, lambda i: (0, 0))
    return pl.pallas_call(
        functools.partial(closure_kernel, steps, feat),
        grid=(steps,),
        in_specs=[
            pl.BlockSpec((16, block), lambda i: (0, i)),
            pl.BlockSpec((16, block), lambda i: (0, i)),
            pl.BlockSpec((1, hid, block), lambda i: (i, 0, 0)),
            pl.BlockSpec((1, hid, block), lambda i: (i, 0, 0)),
            whole((hid, hid)),
            whole((hid, 16)),
            whole((16, hid)),
        ],
        out_specs=[
            pl.BlockSpec((feat, block // 128, 128), lambda i: (0, i, 0)),
            whole((out_rows, hid)),
        ],
        out_shape=[
            jax.ShapeDtypeStruct((feat, cells // 128, 128), jnp.float32),
            jax.ShapeDtypeStruct((out_rows, hid), jnp.float32),
        ],
        scratch_shapes=[
            pltpu.VMEM((hid + 16, block), half),
            pltpu.VMEM((hid + 16, hid), jnp.float32),
            pltpu.VMEM((16, hid), jnp.float32),
            pltpu.VMEM((16, hid), jnp.float32),
        ],
        compiler_params=pltpu.CompilerParams(vmem_limit_bytes=56 << 20),
        name="closure",
    )(sf, sg, act_in, act_mid, w_mid, wo, wi)


def reduce_kernel(rows, cols, factor, g_ref, o_ref, rbuf, cbuf, send_r, recv_r, send_c, recv_c,
                  send_o, recv_o):
    me_r, me_c = lax.axis_index("row"), lax.axis_index("col")
    barrier = pltpu.get_barrier_semaphore()
    for d in range(1, rows):
        pl.semaphore_signal(
            barrier, inc=1, device_id=(lax.rem(me_r + d, rows), me_c), device_id_type=MESH
        )
    for d in range(1, cols):
        pl.semaphore_signal(
            barrier, inc=1, device_id=(me_r, lax.rem(me_c + d, cols)), device_id_type=MESH
        )
    pl.semaphore_wait(barrier, rows + cols - 2)
    first = []
    for d in range(1, rows):
        peer = lax.rem(me_r + d, rows)
        copy = pltpu.make_async_remote_copy(
            src_ref=g_ref.at[peer], dst_ref=rbuf.at[d], send_sem=send_r.at[d],
            recv_sem=recv_r.at[d], device_id=(peer, me_c), device_id_type=MESH,
        )
        copy.start()
        first.append(copy)
    total = g_ref[me_r]
    for d in range(1, rows):
        first[d - 1].wait_recv()
        total = total + rbuf[d]
    cbuf[me_c] = total
    second = []
    for d in range(1, cols):
        copy = pltpu.make_async_remote_copy(
            src_ref=cbuf.at[me_c], dst_ref=cbuf.at[me_c], send_sem=send_c.at[d],
            recv_sem=recv_c.at[d], device_id=(me_r, lax.rem(me_c + d, cols)), device_id_type=MESH,
        )
        copy.start()
        second.append(copy)
    for copy in second:
        copy.wait_recv()
    total = cbuf[0]
    for c in range(1, cols):
        total = total + cbuf[c]
    o_ref[me_r] = total * factor
    third = []
    for d in range(1, rows):
        copy = pltpu.make_async_remote_copy(
            src_ref=o_ref.at[me_r], dst_ref=o_ref.at[me_r], send_sem=send_o.at[d],
            recv_sem=recv_o.at[d], device_id=(lax.rem(me_r + d, rows), me_c), device_id_type=MESH,
        )
        copy.start()
        third.append(copy)
    for copy in third:
        copy.wait_recv()
    for copy in first + second + third:
        copy.wait_send()


def reduce_all(grads, rows, cols, factor):
    _, share, width = grads.shape
    dma = pltpu.SemaphoreType.DMA
    return pl.pallas_call(
        functools.partial(reduce_kernel, rows, cols, factor),
        out_shape=jax.ShapeDtypeStruct(grads.shape, jnp.float32),
        in_specs=[pl.BlockSpec(memory_space=pltpu.VMEM)],
        out_specs=pl.BlockSpec(memory_space=pltpu.VMEM),
        scratch_shapes=[
            pltpu.VMEM((rows, share, width), jnp.float32),
            pltpu.VMEM((cols, share, width), jnp.float32),
            dma((rows,)), dma((rows,)), dma((cols,)), dma((cols,)), dma((rows,)), dma((rows,)),
        ],
        compiler_params=pltpu.CompilerParams(collective_id=0, has_side_effects=True),
        name="reduce_all",
    )(grads)


def per_device(features, cotangent, w_in, bias_in, w_mid, bias_mid, w_out, rows, cols):
    sf, sg, act_in, act_mid = spectral(
        features, cotangent, w_in, bias_in, w_mid, bias_mid, rows, cols
    )
    feat, outs = features.shape[0], w_out.shape[1]
    hid = w_mid.shape[0]
    cells = math.prod(features.shape[1:])
    share = up(hid + 48, 8 * rows) // rows
    field, grads = closure(sf, sg, act_in, act_mid, w_in, w_mid, w_out, rows * share)
    factor = 1.0 / math.sqrt(cells * rows * cols)
    total = reduce_all(grads.reshape(rows, share, hid), rows, cols, factor)
    total = total.reshape(rows * share, hid)
    return (
        field.reshape(features.shape),
        total[hid + 16 : hid + 16 + feat],
        total[hid + 16 + feat],
        total[:hid],
        total[hid + feat],
        total[hid + 32 : hid + 32 + outs].T,
    )


def solution(mesh):
    body = functools.partial(per_device, rows=mesh.shape["row"], cols=mesh.shape["col"])
    return jax.shard_map(
        body,
        mesh=mesh,
        in_specs=(
            P(None, None, "row", "col", None),
            P(None, None, "row", "col", None),
            P(),
            P(),
            P(),
            P(),
            P(),
        ),
        out_specs=(P(None, None, "row", "col", None), P(), P(), P(), P(), P()),
        check_vma=False,
    )
```

```python
import functools
import math

import jax
import jax.numpy as jnp
import numpy as np
from jax import lax
from jax.experimental import pallas as pl
from jax.experimental.pallas import tpu as pltpu
from jax.sharding import PartitionSpec as P

STEP_DT = 0.04
MESH = pl.DeviceIdType.MESH


def kept_modes(length):
    top = (length - 1) // 3
    return top


def padded(values, parts):
    share = -(-len(values) // parts)
    out = np.zeros((parts * share,), np.int64)
    out[: len(values)] = values
    live = np.zeros((parts * share,), np.float64)
    live[: len(values)] = 1.0
    return out.reshape(parts, share), live.reshape(parts, share)


def angles(modes, length):
    pos = np.arange(length)
    turns = (modes[..., None] * pos) % length
    return turns * (2.0 * math.pi / length)


def f32(a):
    return jnp.asarray(np.ascontiguousarray(a), jnp.float32)


def bf16(a):
    return jnp.asarray(np.ascontiguousarray(a), jnp.bfloat16)


def up(value, step):
    return step * (-(-value // step))


class Plan:
    def __init__(self, shape, rows, cols):
        self.nc, _, self.bx, self.by, self.nz = shape
        self.rows, self.cols = rows, cols
        self.nx, self.ny = self.bx * rows, self.by * cols
        self.mz, self.live_z = padded(np.arange(kept_modes(self.nz) + 1), cols)
        top_y, top_x = kept_modes(self.ny), kept_modes(self.nx)
        self.my, self.live_y = padded(np.arange(-top_y, top_y + 1), rows)
        self.mx = np.arange(-top_x, top_x + 1)
        self.kz, self.ky, self.kx = self.mz.shape[1], self.my.shape[1], len(self.mx)
        self.kxp = 8 * (-(-self.kx // 8))
        self.xl = max(d for d in range(1, self.bx + 1) if self.bx % d == 0 and d * self.by <= 128)
        self.xg = self.bx // self.xl
        self.wide = self.xl * self.by
        self.parts = 2 if self.xg % 2 == 0 and (self.bx // 2) % 8 == 0 else 1
        self.hg, self.hx = self.xg // self.parts, self.bx // self.parts
        self.gp = self.nc * self.hg
        while (self.kz * self.gp * self.xl) % 8:
            self.gp += 1
        self.modes = up(2 * self.kz, 8)
        self.rows1 = up(2 * self.kz * self.gp, 8)
        self.rows2 = self.nc * 2 * self.hx
        self.nf, self.ns = 4, 5
        self.rows3 = self.nf * 2 * self.hx
        self.sx = self.ns * self.hg
        self.rows4 = up(2 * self.kz * self.sx, 8)
        self.lines = self.bx * self.by

    def tables(self):
        kz, ky, kx, kxp = self.kz, self.ky, self.kx, self.kxp
        rows, cols, bx, by = self.rows, self.cols, self.bx, self.by
        az = angles(self.mz, self.nz)
        lz = self.live_z[..., None]
        t1 = np.zeros((cols, self.modes, self.nz))
        t1[:, :kz] = np.cos(az) * lz
        t1[:, kz : 2 * kz] = -np.sin(az) * lz
        weight = np.where(self.mz == 0, 1.0, 2.0)[..., None] * lz / self.nz
        t6 = np.zeros((cols, self.modes, self.nz))
        t6[:, :kz] = np.cos(az) * weight
        t6[:, kz : 2 * kz] = -np.sin(az) * weight
        ay = angles(self.my, self.ny)
        cy = np.cos(ay) * self.live_y[..., None]
        sy = np.sin(ay) * self.live_y[..., None]
        t2 = np.zeros((rows, 2, self.ny, 2, 128))
        t5 = np.zeros((rows, 2, 128, 2, self.ny))
        for k in range(ky):
            at = k * kz
            t2[:, 0, :, 0, at] = cy[:, k]
            t2[:, 1, :, 0, at] = sy[:, k]
            t2[:, 0, :, 1, at] = -sy[:, k]
            t2[:, 1, :, 1, at] = cy[:, k]
            t5[:, 0, at, 0] = cy[:, k] / self.ny
            t5[:, 1, at, 0] = -sy[:, k] / self.ny
            t5[:, 0, at, 1] = sy[:, k] / self.ny
            t5[:, 1, at, 1] = cy[:, k] / self.ny
        ax = angles(self.mx, self.nx)
        cx, sx = np.cos(ax), np.sin(ax)
        parts, hx = self.parts, self.hx
        t3 = np.zeros((2, kxp, rows, 2, bx))
        t4 = np.zeros((rows, 2, bx, 2, kxp))
        cr, sr = cx.reshape(kx, rows, bx), sx.reshape(kx, rows, bx)
        t3[0, :kx, :, 0] = cr
        t3[0, :kx, :, 1] = sr
        t3[1, :kx, :, 0] = -sr
        t3[1, :kx, :, 1] = cr
        scale = STEP_DT / self.nx
        ci, si = cr.transpose(1, 2, 0) * scale, sr.transpose(1, 2, 0) * scale
        t4[:, 0, :, 0, :kx] = -si
        t4[:, 0, :, 1, :kx] = -ci
        t4[:, 1, :, 0, :kx] = ci
        t4[:, 1, :, 1, :kx] = -si
        t3 = t3.reshape(2, kxp, rows, 2, parts, hx).transpose(0, 1, 4, 2, 3, 5)
        t4 = t4.reshape(rows, 2, parts, hx, 2, kxp).transpose(2, 0, 1, 3, 4, 5)
        lane_y = np.zeros((rows, 1, 128))
        lane_z = np.zeros((cols, 1, 128))
        lane_y[:, 0, : ky * kz] = np.repeat(self.my, kz, axis=1)
        lane_z[:, 0, : ky * kz] = np.tile(self.mz, (1, ky))
        wave_x = np.zeros((kxp, 128))
        wave_x[:kx] = self.mx[:, None]
        return (
            bf16(t1.reshape(cols * self.modes, self.nz)),
            bf16(t2.reshape(rows, 2 * self.ny, 256)),
            bf16(t3.reshape(2 * kxp, rows * 2 * bx)),
            bf16(t4.reshape(parts, rows * 2 * hx, 2 * kxp)),
            bf16(t5.reshape(rows * 256, 2 * self.ny)),
            bf16(t6.reshape(cols * self.modes, self.nz)),
            f32(wave_x),
            f32(lane_y),
            f32(lane_z),
        )


def spectral_kernel(p, fp, cot, feat, win_ref, bin_ref, wmid_ref, bmid_ref,
                    t1, t2, t3, t4, t5, t6, wx_ref, wy_ref, wz_ref,
                    sf_out, sg_out, act_in, act_mid,
                    s1, d1, s2, d2, s3, d3, s4, d4, e2, q5, o5, flat, abuf, mbuf,
                    w1_ref, w2_ref, b2_ref,
                    send1, recv1, send2, recv2, send3, recv3, send4, recv4, sem_a, sem_m):
    me_r, me_c = lax.axis_index("row"), lax.axis_index("col")
    rows, cols, kz, ky, kxp = p.rows, p.cols, p.kz, p.ky, p.kxp
    bx, by, nc, hx, parts = p.bx, p.by, p.nc, p.hx, p.parts
    last = (((1,), (1,)), ((), ()))
    first = (((0,), (0,)), ((), ()))
    half = jnp.bfloat16

    def row_peer(d):
        return lax.rem(me_r + d, rows)

    def col_peer(d):
        return lax.rem(me_c + d, cols)

    barrier = pltpu.get_barrier_semaphore()
    for d in range(1, rows):
        pl.semaphore_signal(barrier, inc=1, device_id=(row_peer(d), me_c), device_id_type=MESH)
    for d in range(1, cols):
        pl.semaphore_signal(barrier, inc=1, device_id=(me_r, col_peer(d)), device_id_type=MESH)
    sends = []

    def over_col(h, src, dst, send, recv):
        copies = []
        for d in range(1, cols):
            copy = pltpu.make_async_remote_copy(
                src_ref=src.at[h, col_peer(d)], dst_ref=dst.at[h, me_c], send_sem=send.at[h, d],
                recv_sem=recv.at[h, d], device_id=(me_r, col_peer(d)), device_id_type=MESH,
            )
            copy.start()
            copies.append(copy)
        dst[h, me_c] = src[h, me_c]
        sends.extend(copies)
        return copies

    def over_row(h, src, dst, send, recv):
        copies = []
        for d in range(1, rows):
            copy = pltpu.make_async_remote_copy(
                src_ref=src.at[h, row_peer(d)], dst_ref=dst.at[h, me_r], send_sem=send.at[h, d],
                recv_sem=recv.at[h, d], device_id=(row_peer(d), me_c), device_id_type=MESH,
            )
            copy.start()
            copies.append(copy)
        dst[h, me_r] = src[h, me_r]
        sends.extend(copies)
        return copies

    def arrived(copies):
        for copy in copies:
            copy.wait_recv()

    steps, _, block = act_in.shape
    done = [0]

    def keep(i, slot):
        return (
            pltpu.make_async_copy(abuf.at[slot], act_in.at[i], sem_a.at[slot]),
            pltpu.make_async_copy(mbuf.at[slot], act_mid.at[i], sem_m.at[slot]),
        )

    def forward_block(i, carry):
        slot = lax.rem(i, 2)

        @pl.when(i >= 2)
        def _():
            for copy in keep(i, slot):
                copy.wait()

        src = sf_out[:, pl.ds(pl.multiple_of(i * block, block), block)]
        pre = jnp.dot(w1_ref[...], src, preferred_element_type=jnp.float32)
        act = jnp.tanh(pre).astype(half)
        abuf[slot] = act
        pre = jnp.dot(w2_ref[...], act, preferred_element_type=jnp.float32) + b2_ref[:, :1]
        mbuf[slot] = jnp.tanh(pre).astype(half)
        for copy in keep(i, slot):
            copy.start()
        return carry

    def forward(share):
        upto = min(steps, -(-steps * share // 16))
        if upto > done[0]:
            lax.fori_loop(done[0], upto, forward_block, 0)
            done[0] = upto

    def stage1(h):
        for v in range(nc):
            for g in range(p.hg):
                at = v * p.xg + h * p.hg + g
                a = cot[pl.ds(at * p.wide, p.wide), :].astype(half)
                part = lax.dot_general(t1[...], a, last, preferred_element_type=jnp.float32)
                for c in range(cols):
                    s1[h, c, pl.ds(v * p.hg + g, 2 * kz, stride=p.gp), pl.ds(0, p.wide)] = part[
                        c * p.modes : c * p.modes + 2 * kz
                    ]

    def stage2(h):
        count = kz * p.gp
        where = lax.broadcasted_iota(jnp.int32, (count, 128), 1) // by
        for ri in range(2):
            for j in range(p.xl):
                whole = None
                for c in range(cols):
                    tile = d1[h, c, pl.ds(ri * count, count), :]
                    shift = ((c - j) * by) % 128
                    tile = tile if shift == 0 else pltpu.roll(tile, shift, 1)
                    whole = tile if whole is None else jnp.where(where == c, tile, whole)
                e2[ri, pl.ds(j, count, stride=p.xl), :] = whole
        lhs = jnp.concatenate([e2[0].astype(half), e2[1].astype(half)], axis=1)
        per = p.gp * p.xl
        for r in range(rows):
            part = jnp.dot(lhs, t2[r], preferred_element_type=jnp.float32)
            for ri in range(2):
                total = part[:per, ri * 128 : (ri + 1) * 128]
                for k in range(1, kz):
                    total = total + pltpu.roll(
                        part[k * per : (k + 1) * per, ri * 128 : (ri + 1) * 128], k, 1
                    )
                for v in range(nc):
                    s2[h, r, pl.ds((2 * v + ri) * hx, hx), :] = total[v * hx : (v + 1) * hx]

    def stage3():
        wx, wy, wz = wx_ref[...], wy_ref[me_r], wz_ref[me_c]
        vel = []
        for v in range(nc):
            data = jnp.concatenate(
                [d2[h, r, pl.ds(2 * v * hx, 2 * hx), :] for h in range(parts) for r in range(rows)],
                axis=0,
            )
            hat = jnp.dot(t3[...], data.astype(half), preferred_element_type=jnp.float32)
            vel.append((hat[:kxp], hat[kxp:]))
        inverse = 1.0 / jnp.maximum(wx * wx + wy * wy + wz * wz, 1.0)
        fields = [[], [], [], []]
        for ri in range(2):
            inner = (wx * vel[0][ri] + wy * vel[1][ri] + wz * vel[2][ri]) * inverse
            px = vel[0][ri] - wx * inner
            py = vel[1][ri] - wy * inner
            pz = vel[2][ri] - wz * inner
            fields[0].append(py)
            fields[1].append(pz)
            fields[2].append(wy * px + wx * py)
            fields[3].append(wz * px + wx * pz)
        return [jnp.concatenate(field, axis=0).astype(half) for field in fields]

    def stage4(h, fields):
        for f in range(p.nf):
            part = jnp.dot(t4[h], fields[f], preferred_element_type=jnp.float32)
            for r in range(rows):
                s3[h, r, pl.ds(f * 2 * hx, 2 * hx), :] = part[r * 2 * hx : (r + 1) * 2 * hx]

    def stage5(h):
        span = p.ns * hx
        for r in range(rows):
            wy, wz = wy_ref[r], wz_ref[me_c]
            for ri in range(2):
                qy, qz, xy, xz = [d3[h, r, pl.ds((2 * f + ri) * hx, hx), :] for f in range(p.nf)]
                data = jnp.concatenate([wy * qy, wz * qz, xy, xz, wz * qy + wy * qz], axis=0)
                for k in range(kz):
                    tile = data if k == 0 else pltpu.roll(data, 128 - k, 1)
                    q5[pl.ds(k * span, span), pl.ds((2 * r + ri) * 128, 128)] = tile
        part = jnp.dot(q5[...].astype(half), t5[...], preferred_element_type=jnp.float32)
        for ri in range(2):
            o5[ri] = part[:, ri * 128 : (ri + 1) * 128]
        count = kz * p.sx
        where = lax.broadcasted_iota(jnp.int32, (count, 128), 1) // by
        for ri in range(2):
            tiles = [o5[ri, pl.ds(j, count, stride=p.xl), :] for j in range(p.xl)]
            for c in range(cols):
                whole = None
                for j in range(p.xl):
                    shift = ((j - c) * by) % 128
                    tile = tiles[j] if shift == 0 else pltpu.roll(tiles[j], shift, 1)
                    whole = tile if whole is None else jnp.where(where == j, tile, whole)
                s4[h, c, pl.ds(ri * count, count), :] = whole

    def stage6(h):
        pad = jnp.zeros((p.modes - 2 * kz, 128), jnp.float32)
        for g in range(p.hg):
            comps = []
            for comp in range(p.ns):
                pieces = []
                for c in range(cols):
                    pieces.append(d4[h, c, pl.ds(comp * p.hg + g, 2 * kz, stride=p.sx), :])
                    if p.modes > 2 * kz:
                        pieces.append(pad)
                data = jnp.concatenate(pieces, axis=0).astype(half)
                comps.append(
                    lax.dot_general(data, t6[...], first, preferred_element_type=jnp.float32)[
                        : p.wide
                    ]
                )
            order = [-(comps[0] + comps[1]), comps[0], comps[1], comps[2], comps[3], comps[4]]
            line = (h * p.hg + g) * p.wide
            for comp in range(6):
                flat[pl.ds(line * 16 + comp, p.wide, stride=16), :] = order[comp]
            for n in range(p.wide):
                sg_out[:, pl.ds((line + n) * 128, 128)] = flat[
                    pl.ds((line + n) * 16, 16), :
                ].astype(half)

    def take_weights():
        hid = wmid_ref.shape[0]
        bias = bin_ref[...]
        high = bias.astype(half).astype(jnp.float32)
        middle = (bias - high).astype(half).astype(jnp.float32)
        low = bias - high - middle
        rest = jnp.zeros((16 - fp - 3, hid), jnp.float32)
        table = jnp.concatenate(
            [win_ref[...].astype(jnp.float32), high, middle, low, rest], axis=0
        )
        w1_ref[...] = table.T.astype(half)
        w2_ref[...] = wmid_ref[...].astype(jnp.float32).T.astype(half)
        b2_ref[...] = jnp.broadcast_to(bmid_ref[...], (128, hid)).T

    def take_features():
        row = lax.broadcasted_iota(jnp.int32, (p.lines * 16, 128), 0)
        flat[...] = jnp.where((row % 16 >= fp) & (row % 16 < fp + 3), 1.0, 0.0)
        for f in range(fp):
            flat[pl.ds(f, p.lines, stride=16), :] = feat[f].astype(jnp.float32)
        for n in range(p.lines):
            sf_out[:, pl.ds(n * 128, 128)] = flat[pl.ds(n * 16, 16), :].astype(half)
        flat[...] = jnp.zeros_like(flat)

    if p.wide < 128:
        s1[...] = jnp.zeros_like(s1)
    moves1, moves2, moves3, moves4 = [], [], [], []
    for h in range(parts):
        stage1(h)
        if h == 0:
            pl.semaphore_wait(barrier, rows + cols - 2)
        moves1.append(over_col(h, s1, d1, send1, recv1))
    take_weights()
    take_features()
    forward(1)
    for h in range(parts):
        arrived(moves1[h])
        stage2(h)
        moves2.append(over_row(h, s2, d2, send2, recv2))
        forward(3 + 3 * h)
    for h in range(parts):
        arrived(moves2[h])
    fields = stage3()
    for h in range(parts):
        stage4(h, fields)
        moves3.append(over_row(h, s3, d3, send3, recv3))
    forward(10)
    for h in range(parts):
        arrived(moves3[h])
        stage5(h)
        moves4.append(over_col(h, s4, d4, send4, recv4))
        forward(13 + 3 * h)
    forward(16)
    for h in range(parts):
        arrived(moves4[h])
        stage6(h)
    for i in range(max(0, steps - 2), steps):
        for copy in keep(i, i % 2):
            copy.wait()
    for copy in sends:
        copy.wait_send()


def spectral(features, cotangent, w_in, bias_in, w_mid, bias_mid, rows, cols):
    p = Plan(cotangent.shape, rows, cols)
    feat, hid = w_in.shape
    cells = p.lines * p.nz
    block = math.gcd(cells, 4096)
    steps = cells // block
    dma = pltpu.SemaphoreType.DMA
    vmem = pl.BlockSpec(memory_space=pltpu.VMEM)
    hbm = pl.BlockSpec(memory_space=pl.ANY)
    single, half = jnp.float32, jnp.bfloat16
    parts = p.parts
    return pl.pallas_call(
        functools.partial(spectral_kernel, p, feat),
        out_shape=[
            jax.ShapeDtypeStruct((16, cells), half),
            jax.ShapeDtypeStruct((16, cells), half),
            jax.ShapeDtypeStruct((steps, hid, block), half),
            jax.ShapeDtypeStruct((steps, hid, block), half),
        ],
        in_specs=[vmem] * 15,
        out_specs=[vmem, vmem, hbm, hbm],
        scratch_shapes=[
            pltpu.VMEM((parts, cols, p.rows1, 128), single),
            pltpu.VMEM((parts, cols, p.rows1, 128), single),
            pltpu.VMEM((parts, rows, p.rows2, 128), single),
            pltpu.VMEM((parts, rows, p.rows2, 128), single),
            pltpu.VMEM((parts, rows, p.rows3, 128), single),
            pltpu.VMEM((parts, rows, p.rows3, 128), single),
            pltpu.VMEM((parts, cols, p.rows4, 128), single),
            pltpu.VMEM((parts, cols, p.rows4, 128), single),
            pltpu.VMEM((2, p.kz * p.gp * p.xl, 128), single),
            pltpu.VMEM((p.kz * p.ns * p.hx, rows * 256), single),
            pltpu.VMEM((2, p.kz * p.ns * p.hx, 128), single),
            pltpu.VMEM((p.lines * 16, 128), single),
            pltpu.VMEM((2, hid, block), half),
            pltpu.VMEM((2, hid, block), half),
            pltpu.VMEM((hid, 16), half),
            pltpu.VMEM((hid, hid), half),
            pltpu.VMEM((hid, 128), single),
            dma((parts, cols)), dma((parts, cols)), dma((parts, rows)), dma((parts, rows)),
            dma((parts, rows)), dma((parts, rows)), dma((parts, cols)), dma((parts, cols)),
            dma((2,)), dma((2,)),
        ],
        compiler_params=pltpu.CompilerParams(
            collective_id=1, has_side_effects=True, vmem_limit_bytes=56 << 20
        ),
        name="spectral",
    )(
        cotangent.reshape(p.nc * p.lines, p.nz), features.reshape(feat, p.lines, p.nz),
        w_in, bias_in[None], w_mid, bias_mid[None], *p.tables(),
    )


def closure_kernel(steps, feat, sf_ref, sg_ref, ai_ref, am_ref, w2_ref, wout_ref, win_ref,
                   gx_ref, out_ref, cat, accm, acci, acco, wo_ref, wi_ref, wide_ref):
    step = pl.program_id(0)
    hid, block = ai_ref.shape[1:]
    half = jnp.bfloat16
    last = (((1,), (1,)), ((), ()))

    @pl.when(step == 0)
    def _():
        accm[...] = jnp.zeros_like(accm)
        acci[...] = jnp.zeros_like(acci)
        acco[...] = jnp.zeros_like(acco)
        fp, outs = win_ref.shape[0], wout_ref.shape[1]
        rest = jnp.zeros((16 - fp, hid), jnp.float32)
        wi_ref[...] = jnp.concatenate(
            [win_ref[...].astype(jnp.float32), rest], axis=0
        ).astype(half)
        wide_ref[...] = jnp.zeros_like(wide_ref)
        wide_ref[:, pl.ds(0, outs)] = wout_ref[...].astype(jnp.float32)
        wo_ref[...] = wide_ref[:, :16].astype(half)

    sf, sg = sf_ref[...], sg_ref[...]
    act_mid = am_ref[0]
    cat[pl.ds(0, hid), :] = ai_ref[0]
    cat[pl.ds(hid, 16), :] = sf
    back = jnp.dot(wo_ref[...], sg, preferred_element_type=jnp.float32)
    wide = act_mid.astype(jnp.float32)
    delta_mid = (back * (1.0 - wide * wide)).astype(half)
    acco[...] += lax.dot_general(sg, act_mid, last, preferred_element_type=jnp.float32)
    accm[...] += lax.dot_general(cat[...], delta_mid, last, preferred_element_type=jnp.float32)
    back = jnp.dot(w2_ref[...], delta_mid, preferred_element_type=jnp.float32)
    wide = ai_ref[0].astype(jnp.float32)
    delta_in = (back * (1.0 - wide * wide)).astype(half)
    acci[...] += lax.dot_general(sf, delta_in, last, preferred_element_type=jnp.float32)
    grad = jnp.dot(wi_ref[...], delta_in, preferred_element_type=jnp.float32)
    for row in range(gx_ref.shape[1]):
        gx_ref[:, row, :] = grad[:feat, row * 128 : (row + 1) * 128]

    @pl.when(step == steps - 1)
    def _():
        out_ref[...] = jnp.zeros_like(out_ref)
        for side in range(2):
            lanes = slice(side * (hid // 2), (side + 1) * (hid // 2))
            out_ref[side, pl.ds(0, hid + 16), :] = accm[:, lanes]
            out_ref[side, pl.ds(hid + 16, 16), :] = acci[:, lanes]
            out_ref[side, pl.ds(hid + 32, 16), :] = acco[:, lanes]


def closure(sf, sg, act_in, act_mid, w_in, w_mid, w_out, out_rows):
    steps, hid, block = act_in.shape
    feat, outs = w_in.shape[0], w_out.shape[1]
    cells = steps * block
    half = jnp.bfloat16
    whole = lambda shape: pl.BlockSpec(shape, lambda i: (0, 0))
    return pl.pallas_call(
        functools.partial(closure_kernel, steps, feat),
        grid=(steps,),
        in_specs=[
            pl.BlockSpec((16, block), lambda i: (0, i)),
            pl.BlockSpec((16, block), lambda i: (0, i)),
            pl.BlockSpec((1, hid, block), lambda i: (i, 0, 0)),
            pl.BlockSpec((1, hid, block), lambda i: (i, 0, 0)),
            whole((hid, hid)),
            whole((hid, outs)),
            whole((feat, hid)),
        ],
        out_specs=[
            pl.BlockSpec((feat, block // 128, 128), lambda i: (0, i, 0)),
            pl.BlockSpec((2, out_rows, hid // 2), lambda i: (0, 0, 0)),
        ],
        out_shape=[
            jax.ShapeDtypeStruct((feat, cells // 128, 128), jnp.float32),
            jax.ShapeDtypeStruct((2, out_rows, hid // 2), jnp.float32),
        ],
        scratch_shapes=[
            pltpu.VMEM((hid + 16, block), half),
            pltpu.VMEM((hid + 16, hid), jnp.float32),
            pltpu.VMEM((16, hid), jnp.float32),
            pltpu.VMEM((16, hid), jnp.float32),
            pltpu.VMEM((hid, 16), half),
            pltpu.VMEM((16, hid), half),
            pltpu.VMEM((hid, 128), jnp.float32),
        ],
        compiler_params=pltpu.CompilerParams(vmem_limit_bytes=56 << 20),
        name="closure",
    )(sf, sg, act_in, act_mid, w_mid, w_out, w_in)


def reduce_kernel(rows, cols, factor, g_ref, o_ref, pair, held, parts, total,
                  send_a, recv_a, send_b, recv_b, send_c, recv_c, send_d, recv_d):
    me_r, me_c = lax.axis_index("row"), lax.axis_index("col")
    layers = rows // 2
    core, me_z = lax.rem(me_r, 2), me_r // 2
    other = (me_r + 1 - 2 * core, me_c)
    share = parts.shape[1]

    def peer(dz, dc):
        z, c = lax.rem(me_z + dz, layers), lax.rem(me_c + dc, cols)
        return z, c, (2 * z + core, c)

    def block(z, c):
        return pl.ds(pl.multiple_of((z * cols + c) * share, 8), share)

    steps = [(dz, dc) for dz in range(layers) for dc in range(cols) if dz or dc]
    barrier = pltpu.get_barrier_semaphore()
    pl.semaphore_signal(barrier, inc=1, device_id=other, device_id_type=MESH)
    for dz, dc in steps:
        pl.semaphore_signal(barrier, inc=1, device_id=peer(dz, dc)[2], device_id_type=MESH)
    pl.semaphore_wait(barrier, len(steps) + 1)
    swap = pltpu.make_async_remote_copy(
        src_ref=g_ref.at[1 - core], dst_ref=pair, send_sem=send_a, recv_sem=recv_a,
        device_id=other, device_id_type=MESH,
    )
    swap.start()
    swap.wait_recv()
    held[...] = g_ref[core] + pair[...]
    first = []
    for dz, dc in steps:
        z, c, device = peer(dz, dc)
        at = dz * cols + dc
        copy = pltpu.make_async_remote_copy(
            src_ref=held.at[block(z, c)], dst_ref=parts.at[at], send_sem=send_b.at[at],
            recv_sem=recv_b.at[at], device_id=device, device_id_type=MESH,
        )
        copy.start()
        first.append(copy)
    mine = block(me_z, me_c)
    value = held[mine, :]
    for copy, (dz, dc) in zip(first, steps):
        copy.wait_recv()
        value = value + parts[dz * cols + dc]
    total[mine, :] = value * factor
    second, third = [], []

    def hand_over(at, where):
        copy = pltpu.make_async_remote_copy(
            src_ref=total.at[where], dst_ref=o_ref.at[core, where], send_sem=send_d.at[at],
            recv_sem=recv_d.at[at], device_id=other, device_id_type=MESH,
        )
        copy.start()
        third.append(copy)

    for dz, dc in steps:
        at = dz * cols + dc
        copy = pltpu.make_async_remote_copy(
            src_ref=total.at[mine], dst_ref=total.at[mine], send_sem=send_c.at[at],
            recv_sem=recv_c.at[at], device_id=peer(dz, dc)[2], device_id_type=MESH,
        )
        copy.start()
        second.append(copy)
    hand_over(0, mine)
    for copy, (dz, dc) in zip(second, steps):
        copy.wait_recv()
        z, c, _ = peer(layers - dz, cols - dc)
        hand_over(dz * cols + dc, block(z, c))
    o_ref[core] = total[...]
    for copy in third:
        copy.wait_recv()
    for copy in [swap] + first + second + third:
        copy.wait_send()


def reduce_all(grads, rows, cols, factor):
    _, length, width = grads.shape
    count = rows // 2 * cols
    share = length // count
    dma = pltpu.SemaphoreType.DMA
    buffer = pltpu.VMEM((length, width), jnp.float32)
    return pl.pallas_call(
        functools.partial(reduce_kernel, rows, cols, factor),
        out_shape=jax.ShapeDtypeStruct(grads.shape, jnp.float32),
        in_specs=[pl.BlockSpec(memory_space=pltpu.VMEM)],
        out_specs=pl.BlockSpec(memory_space=pltpu.VMEM),
        scratch_shapes=[
            buffer, buffer, pltpu.VMEM((count, share, width), jnp.float32), buffer,
            dma(()), dma(()), dma((count,)), dma((count,)), dma((count,)), dma((count,)),
            dma((count,)), dma((count,)),
        ],
        compiler_params=pltpu.CompilerParams(collective_id=0, has_side_effects=True),
        name="reduce_all",
    )(grads)


def final_kernel(feat, outs, t_ref, win_ref, bin_ref, wmid_ref, bmid_ref, wout_ref):
    hid = wmid_ref.shape[0]
    side = hid // 2
    for n in range(2):
        lanes = pl.ds(n * side, side)
        wmid_ref[:, lanes] = t_ref[n, pl.ds(0, hid), :]
        bmid_ref[:, lanes] = t_ref[n, pl.ds(hid + feat, 1), :]
        win_ref[:, lanes] = t_ref[n, pl.ds(hid + 16, feat), :]
        bin_ref[:, lanes] = t_ref[n, pl.ds(hid + 16 + feat, 1), :]
        wout_ref[lanes, :] = t_ref[n, pl.ds(hid + 32, 8), :].T[:, :outs]


def final(total, feat, outs, hid):
    vmem = pl.BlockSpec(memory_space=pltpu.VMEM)
    single = jnp.float32
    return pl.pallas_call(
        functools.partial(final_kernel, feat, outs),
        out_shape=[
            jax.ShapeDtypeStruct((feat, hid), single),
            jax.ShapeDtypeStruct((1, hid), single),
            jax.ShapeDtypeStruct((hid, hid), single),
            jax.ShapeDtypeStruct((1, hid), single),
            jax.ShapeDtypeStruct((hid, outs), single),
        ],
        in_specs=[vmem],
        out_specs=[vmem] * 5,
        name="final",
    )(total)


def per_device(features, cotangent, w_in, bias_in, w_mid, bias_mid, w_out, rows, cols):
    sf, sg, act_in, act_mid = spectral(
        features, cotangent, w_in, bias_in, w_mid, bias_mid, rows, cols
    )
    feat, outs = features.shape[0], w_out.shape[1]
    hid = w_mid.shape[0]
    cells = math.prod(features.shape[1:])
    length = up(hid + 48, 8 * (rows // 2) * cols)
    field, grads = closure(sf, sg, act_in, act_mid, w_in, w_mid, w_out, length)
    factor = 1.0 / math.sqrt(cells * rows * cols)
    total = reduce_all(grads, rows, cols, factor)
    g_in, b_in, g_mid, b_mid, g_out = final(total, feat, outs, hid)
    return field.reshape(features.shape), g_in, b_in[0], g_mid, b_mid[0], g_out


def solution(mesh):
    body = functools.partial(per_device, rows=mesh.shape["row"], cols=mesh.shape["col"])
    return jax.shard_map(
        body,
        mesh=mesh,
        in_specs=(
            P(None, None, "row", "col", None),
            P(None, None, "row", "col", None),
            P(),
            P(),
            P(),
            P(),
            P(),
        ),
        out_specs=(P(None, None, "row", "col", None), P(), P(), P(), P(), P()),
        check_vma=False,
    )
```

```python
import functools
import math

import jax
import jax.numpy as jnp
import numpy as np
from jax import lax
from jax.experimental import pallas as pl
from jax.experimental.pallas import tpu as pltpu
from jax.sharding import PartitionSpec as P

STEP_DT = 0.04
MESH = pl.DeviceIdType.MESH


def kept_modes(length):
    top = (length - 1) // 3
    return top


def padded(values, parts):
    share = -(-len(values) // parts)
    out = np.zeros((parts * share,), np.int64)
    out[: len(values)] = values
    live = np.zeros((parts * share,), np.float64)
    live[: len(values)] = 1.0
    return out.reshape(parts, share), live.reshape(parts, share)


def angles(modes, length):
    pos = np.arange(length)
    turns = (modes[..., None] * pos) % length
    return turns * (2.0 * math.pi / length)


def f32(a):
    return jnp.asarray(np.ascontiguousarray(a), jnp.float32)


def bf16(a):
    return jnp.asarray(np.ascontiguousarray(a), jnp.bfloat16)


def up(value, step):
    return step * (-(-value // step))


class Plan:
    def __init__(self, shape, rows, cols):
        self.nc, _, self.bx, self.by, self.nz = shape
        self.rows, self.cols = rows, cols
        self.nx, self.ny = self.bx * rows, self.by * cols
        self.mz, self.live_z = padded(np.arange(kept_modes(self.nz) + 1), cols)
        top_y, top_x = kept_modes(self.ny), kept_modes(self.nx)
        self.my, self.live_y = padded(np.arange(-top_y, top_y + 1), rows)
        self.mx = np.arange(-top_x, top_x + 1)
        self.kz, self.ky, self.kx = self.mz.shape[1], self.my.shape[1], len(self.mx)
        self.kxp = 8 * (-(-self.kx // 8))
        self.xl = max(d for d in range(1, self.bx + 1) if self.bx % d == 0 and d * self.by <= 128)
        self.xg = self.bx // self.xl
        self.wide = self.xl * self.by
        self.parts = 2 if self.xg % 2 == 0 and (self.bx // 2) % 8 == 0 else 1
        self.hg, self.hx = self.xg // self.parts, self.bx // self.parts
        self.gp = self.nc * self.hg
        while (self.kz * self.gp * self.xl) % 8:
            self.gp += 1
        self.modes = up(2 * self.kz, 8)
        self.rows1 = up(2 * self.kz * self.gp, 8)
        self.rows2 = self.nc * 2 * self.hx
        self.nf, self.ns = 4, 5
        self.rows3 = self.nf * 2 * self.hx
        self.sx = self.ns * self.hg
        self.rows4 = up(2 * self.kz * self.sx, 8)
        self.lines = self.bx * self.by

    def tables(self):
        kz, ky, kx, kxp = self.kz, self.ky, self.kx, self.kxp
        rows, cols, bx, by = self.rows, self.cols, self.bx, self.by
        az = angles(self.mz, self.nz)
        lz = self.live_z[..., None]
        t1 = np.zeros((cols, self.modes, self.nz))
        t1[:, :kz] = np.cos(az) * lz
        t1[:, kz : 2 * kz] = -np.sin(az) * lz
        weight = np.where(self.mz == 0, 1.0, 2.0)[..., None] * lz / self.nz
        t6 = np.zeros((cols, self.modes, self.nz))
        t6[:, :kz] = np.cos(az) * weight
        t6[:, kz : 2 * kz] = -np.sin(az) * weight
        ay = angles(self.my, self.ny)
        cy = np.cos(ay) * self.live_y[..., None]
        sy = np.sin(ay) * self.live_y[..., None]
        t2 = np.zeros((rows, 2, self.ny, 2, 128))
        t5 = np.zeros((rows, 2, 128, 2, self.ny))
        for k in range(ky):
            at = k * kz
            t2[:, 0, :, 0, at] = cy[:, k]
            t2[:, 1, :, 0, at] = sy[:, k]
            t2[:, 0, :, 1, at] = -sy[:, k]
            t2[:, 1, :, 1, at] = cy[:, k]
            t5[:, 0, at, 0] = cy[:, k] / self.ny
            t5[:, 1, at, 0] = -sy[:, k] / self.ny
            t5[:, 0, at, 1] = sy[:, k] / self.ny
            t5[:, 1, at, 1] = cy[:, k] / self.ny
        ax = angles(self.mx, self.nx)
        cx, sx = np.cos(ax), np.sin(ax)
        parts, hx = self.parts, self.hx
        t3 = np.zeros((2, kxp, rows, 2, bx))
        t4 = np.zeros((rows, 2, bx, 2, kxp))
        cr, sr = cx.reshape(kx, rows, bx), sx.reshape(kx, rows, bx)
        t3[0, :kx, :, 0] = cr
        t3[0, :kx, :, 1] = sr
        t3[1, :kx, :, 0] = -sr
        t3[1, :kx, :, 1] = cr
        scale = STEP_DT / self.nx
        ci, si = cr.transpose(1, 2, 0) * scale, sr.transpose(1, 2, 0) * scale
        t4[:, 0, :, 0, :kx] = -si
        t4[:, 0, :, 1, :kx] = -ci
        t4[:, 1, :, 0, :kx] = ci
        t4[:, 1, :, 1, :kx] = -si
        t3 = t3.reshape(2, kxp, rows, 2, parts, hx).transpose(0, 1, 4, 2, 3, 5)
        t4 = t4.reshape(rows, 2, parts, hx, 2, kxp).transpose(2, 0, 1, 3, 4, 5)
        lane_y = np.zeros((rows, 1, 128))
        lane_z = np.zeros((cols, 1, 128))
        lane_y[:, 0, : ky * kz] = np.repeat(self.my, kz, axis=1)
        lane_z[:, 0, : ky * kz] = np.tile(self.mz, (1, ky))
        wave_x = np.zeros((kxp, 128))
        wave_x[:kx] = self.mx[:, None]
        return (
            bf16(t1.reshape(cols * self.modes, self.nz)),
            bf16(t2.reshape(rows, 2 * self.ny, 256)),
            bf16(t3.reshape(2 * kxp, rows * 2 * bx)),
            bf16(t4.reshape(parts, rows * 2 * hx, 2 * kxp)),
            bf16(t5.reshape(rows * 256, 2 * self.ny)),
            bf16(t6.reshape(cols * self.modes, self.nz)),
            f32(wave_x),
            f32(lane_y),
            f32(lane_z),
        )


def whole_kernel(p, fp, factor, cot, feat, win_ref, bin_ref, wmid_ref, bmid_ref, wout_ref,
                    t1, t2, t3, t4, t5, t6, wx_ref, wy_ref, wz_ref,
                    gx_ref, o_ref, act_in, act_mid,
                    s1, d1, s2, d2, s3, d3, s4, d4, e2, q5, o5, flat, abuf, mbuf,
                    w1_ref, w2_ref, b2_ref, wi_ref, wo_ref, sf_out, sg_out, accm, acci, acco,
                    grads, pair, held, pieces, total,
                    send1, recv1, send2, recv2, send3, recv3, send4, recv4, sem_a, sem_m,
                    load_a, load_m, send_a, recv_a, send_b, recv_b, send_c, recv_c,
                    send_d, recv_d):
    me_r, me_c = lax.axis_index("row"), lax.axis_index("col")
    rows, cols, kz, ky, kxp = p.rows, p.cols, p.kz, p.ky, p.kxp
    bx, by, nc, hx, parts = p.bx, p.by, p.nc, p.hx, p.parts
    last = (((1,), (1,)), ((), ()))
    first = (((0,), (0,)), ((), ()))
    half = jnp.bfloat16

    def row_peer(d):
        return lax.rem(me_r + d, rows)

    def col_peer(d):
        return lax.rem(me_c + d, cols)

    barrier = pltpu.get_barrier_semaphore()
    for d in range(1, rows):
        pl.semaphore_signal(barrier, inc=1, device_id=(row_peer(d), me_c), device_id_type=MESH)
    for d in range(1, cols):
        pl.semaphore_signal(barrier, inc=1, device_id=(me_r, col_peer(d)), device_id_type=MESH)
    layers = rows // 2
    core, me_z = lax.rem(me_r, 2), me_r // 2
    other = (me_r + 1 - 2 * core, me_c)
    share = pieces.shape[1]

    def chip(dz, dc):
        z, c = lax.rem(me_z + dz, layers), lax.rem(me_c + dc, cols)
        return z, c, (2 * z + core, c)

    def place(z, c):
        return pl.ds(pl.multiple_of((z * cols + c) * share, 8), share)

    chips = [(dz, dc) for dz in range(layers) for dc in range(cols) if dz or dc]
    greeted = rows + cols - 2
    for dz, dc in chips:
        if dz and dc:
            greeted += 1
            pl.semaphore_signal(barrier, inc=1, device_id=chip(dz, dc)[2], device_id_type=MESH)
    sends = []

    def over_col(h, src, dst, send, recv):
        copies = []
        for d in range(1, cols):
            copy = pltpu.make_async_remote_copy(
                src_ref=src.at[h, col_peer(d)], dst_ref=dst.at[h, me_c], send_sem=send.at[h, d],
                recv_sem=recv.at[h, d], device_id=(me_r, col_peer(d)), device_id_type=MESH,
            )
            copy.start()
            copies.append(copy)
        dst[h, me_c] = src[h, me_c]
        sends.extend(copies)
        return copies

    def over_row(h, src, dst, send, recv):
        copies = []
        for d in range(1, rows):
            copy = pltpu.make_async_remote_copy(
                src_ref=src.at[h, row_peer(d)], dst_ref=dst.at[h, me_r], send_sem=send.at[h, d],
                recv_sem=recv.at[h, d], device_id=(row_peer(d), me_c), device_id_type=MESH,
            )
            copy.start()
            copies.append(copy)
        dst[h, me_r] = src[h, me_r]
        sends.extend(copies)
        return copies

    def arrived(copies):
        for copy in copies:
            copy.wait_recv()

    steps, hid, block = act_in.shape
    inner = math.gcd(block, 512)
    done = [0]

    def keep(i, slot):
        return (
            pltpu.make_async_copy(
                abuf.at[slot, pl.ds(0, hid)], act_in.at[i], sem_a.at[slot]
            ),
            pltpu.make_async_copy(mbuf.at[slot], act_mid.at[i], sem_m.at[slot]),
        )

    def forward_block(i, carry):
        slot = lax.rem(i, 2)

        @pl.when(i >= 2)
        def _():
            for copy in keep(i, slot):
                copy.wait()

        src = sf_out[:, pl.ds(pl.multiple_of(i * block, block), block)]
        pre = jnp.dot(w1_ref[...], src, preferred_element_type=jnp.float32)
        act = jnp.tanh(pre).astype(half)
        abuf[slot, pl.ds(0, hid), :] = act
        pre = jnp.dot(w2_ref[...], act, preferred_element_type=jnp.float32) + b2_ref[:, :1]
        mbuf[slot] = jnp.tanh(pre).astype(half)
        for copy in keep(i, slot):
            copy.start()
        return carry

    def fetch(i, slot):
        return (
            pltpu.make_async_copy(
                act_in.at[i], abuf.at[slot, pl.ds(0, hid)], load_a.at[slot]
            ),
            pltpu.make_async_copy(act_mid.at[i], mbuf.at[slot], load_m.at[slot]),
        )

    def backward_block(i, carry):
        slot = lax.rem(i, 2)
        for copy in fetch(i, slot):
            copy.wait()
        start = pl.multiple_of(i * block, block)
        abuf[slot, pl.ds(hid, 16), :] = sf_out[:, pl.ds(start, block)]
        back_mid, delta_mid, back_in, delta_in = {}, {}, {}, {}

        def lanes(n):
            return pl.ds(n * inner, inner)

        def source(ref, n):
            return ref[:, pl.ds(pl.multiple_of(start + n * inner, inner), inner)]

        def gate(back, act):
            wide = act.astype(jnp.float32)
            return (back * (1.0 - wide * wide)).astype(half)

        def enter(n):
            sg, act = source(sg_out, n), mbuf[slot, :, lanes(n)]
            acco[...] += lax.dot_general(sg, act, last, preferred_element_type=jnp.float32)
            back_mid[n] = jnp.dot(wo_ref[...], sg, preferred_element_type=jnp.float32)

        def middle(n):
            delta_mid[n] = gate(back_mid.pop(n), mbuf[slot, :, lanes(n)])

        def weigh(n):
            delta = delta_mid.pop(n)
            back_in[n] = jnp.dot(wmid_ref[...], delta, preferred_element_type=jnp.float32)
            accm[...] += lax.dot_general(
                abuf[slot, :, lanes(n)], delta, last, preferred_element_type=jnp.float32
            )

        def lower(n):
            delta_in[n] = gate(back_in.pop(n), abuf[slot, pl.ds(0, hid), lanes(n)])

        def leave(n):
            delta = delta_in.pop(n)
            acci[...] += lax.dot_general(
                source(sf_out, n), delta, last, preferred_element_type=jnp.float32
            )
            grad = jnp.dot(wi_ref[...], delta, preferred_element_type=jnp.float32)
            for row in range(inner // 128):
                line = i * (block // 128) + n * (inner // 128) + row
                gx_ref[:, line, :] = grad[:fp, row * 128 : (row + 1) * 128]

        count = block // inner
        for turn in range(count + 4):
            for late, work in ((4, leave), (3, lower), (2, weigh), (1, middle), (0, enter)):
                if 0 <= turn - late < count:
                    work(turn - late)

        @pl.when(i + 2 < steps)
        def _():
            for copy in fetch(i + 2, slot):
                copy.start()

        return carry

    def forward(share):
        upto = min(steps, -(-steps * share // 16))
        if upto > done[0]:
            lax.fori_loop(done[0], upto, forward_block, 0)
            done[0] = upto

    def stage1(h):
        for v in range(nc):
            for g in range(p.hg):
                at = v * p.xg + h * p.hg + g
                a = cot[pl.ds(at * p.wide, p.wide), :].astype(half)
                part = lax.dot_general(t1[...], a, last, preferred_element_type=jnp.float32)
                for c in range(cols):
                    s1[h, c, pl.ds(v * p.hg + g, 2 * kz, stride=p.gp), pl.ds(0, p.wide)] = part[
                        c * p.modes : c * p.modes + 2 * kz
                    ]

    def stage2(h):
        count = kz * p.gp
        where = lax.broadcasted_iota(jnp.int32, (count, 128), 1) // by
        for ri in range(2):
            for j in range(p.xl):
                whole = None
                for c in range(cols):
                    tile = d1[h, c, pl.ds(ri * count, count), :]
                    shift = ((c - j) * by) % 128
                    tile = tile if shift == 0 else pltpu.roll(tile, shift, 1)
                    whole = tile if whole is None else jnp.where(where == c, tile, whole)
                e2[ri, pl.ds(j, count, stride=p.xl), :] = whole
        lhs = jnp.concatenate([e2[0].astype(half), e2[1].astype(half)], axis=1)
        per = p.gp * p.xl
        for r in range(rows):
            part = jnp.dot(lhs, t2[r], preferred_element_type=jnp.float32)
            for ri in range(2):
                total = part[:per, ri * 128 : (ri + 1) * 128]
                for k in range(1, kz):
                    total = total + pltpu.roll(
                        part[k * per : (k + 1) * per, ri * 128 : (ri + 1) * 128], k, 1
                    )
                for v in range(nc):
                    s2[h, r, pl.ds((2 * v + ri) * hx, hx), :] = total[v * hx : (v + 1) * hx]

    def stage3():
        wx, wy, wz = wx_ref[...], wy_ref[me_r], wz_ref[me_c]
        vel = []
        for v in range(nc):
            data = jnp.concatenate(
                [d2[h, r, pl.ds(2 * v * hx, 2 * hx), :] for h in range(parts) for r in range(rows)],
                axis=0,
            )
            hat = jnp.dot(t3[...], data.astype(half), preferred_element_type=jnp.float32)
            vel.append((hat[:kxp], hat[kxp:]))
        inverse = 1.0 / jnp.maximum(wx * wx + wy * wy + wz * wz, 1.0)
        fields = [[], [], [], []]
        for ri in range(2):
            inner = (wx * vel[0][ri] + wy * vel[1][ri] + wz * vel[2][ri]) * inverse
            px = vel[0][ri] - wx * inner
            py = vel[1][ri] - wy * inner
            pz = vel[2][ri] - wz * inner
            fields[0].append(py)
            fields[1].append(pz)
            fields[2].append(wy * px + wx * py)
            fields[3].append(wz * px + wx * pz)
        return [jnp.concatenate(field, axis=0).astype(half) for field in fields]

    def stage4(h, fields):
        for f in range(p.nf):
            part = jnp.dot(t4[h], fields[f], preferred_element_type=jnp.float32)
            for r in range(rows):
                s3[h, r, pl.ds(f * 2 * hx, 2 * hx), :] = part[r * 2 * hx : (r + 1) * 2 * hx]

    def stage5(h):
        span = p.ns * hx
        for r in range(rows):
            wy, wz = wy_ref[r], wz_ref[me_c]
            for ri in range(2):
                qy, qz, xy, xz = [d3[h, r, pl.ds((2 * f + ri) * hx, hx), :] for f in range(p.nf)]
                data = jnp.concatenate([wy * qy, wz * qz, xy, xz, wz * qy + wy * qz], axis=0)
                for k in range(kz):
                    tile = data if k == 0 else pltpu.roll(data, 128 - k, 1)
                    q5[pl.ds(k * span, span), pl.ds((2 * r + ri) * 128, 128)] = tile
        part = jnp.dot(q5[...].astype(half), t5[...], preferred_element_type=jnp.float32)
        for ri in range(2):
            o5[ri] = part[:, ri * 128 : (ri + 1) * 128]
        count = kz * p.sx
        where = lax.broadcasted_iota(jnp.int32, (count, 128), 1) // by
        for ri in range(2):
            tiles = [o5[ri, pl.ds(j, count, stride=p.xl), :] for j in range(p.xl)]
            for c in range(cols):
                whole = None
                for j in range(p.xl):
                    shift = ((j - c) * by) % 128
                    tile = tiles[j] if shift == 0 else pltpu.roll(tiles[j], shift, 1)
                    whole = tile if whole is None else jnp.where(where == j, tile, whole)
                s4[h, c, pl.ds(ri * count, count), :] = whole

    def stage6(h):
        pad = jnp.zeros((p.modes - 2 * kz, 128), jnp.float32)
        for g in range(p.hg):
            comps = []
            for comp in range(p.ns):
                pieces = []
                for c in range(cols):
                    pieces.append(d4[h, c, pl.ds(comp * p.hg + g, 2 * kz, stride=p.sx), :])
                    if p.modes > 2 * kz:
                        pieces.append(pad)
                data = jnp.concatenate(pieces, axis=0).astype(half)
                comps.append(
                    lax.dot_general(data, t6[...], first, preferred_element_type=jnp.float32)[
                        : p.wide
                    ]
                )
            order = [-(comps[0] + comps[1]), comps[0], comps[1], comps[2], comps[3], comps[4]]
            line = (h * p.hg + g) * p.wide
            for comp in range(6):
                flat[pl.ds(line * 16 + comp, p.wide, stride=16), :] = order[comp]
            for n in range(p.wide):
                sg_out[:, pl.ds((line + n) * 128, 128)] = flat[
                    pl.ds((line + n) * 16, 16), :
                ].astype(half)

    def take_weights():
        bias = bin_ref[...]
        high = bias.astype(half).astype(jnp.float32)
        middle = (bias - high).astype(half).astype(jnp.float32)
        low = bias - high - middle
        rest = jnp.zeros((16 - fp - 3, hid), jnp.float32)
        table = jnp.concatenate(
            [win_ref[...].astype(jnp.float32), high, middle, low, rest], axis=0
        )
        w1_ref[...] = table.T.astype(half)
        w2_ref[...] = wmid_ref[...].astype(jnp.float32).T.astype(half)
        b2_ref[...] = jnp.broadcast_to(bmid_ref[...], (128, hid)).T
        outs = wout_ref.shape[0]
        rest = jnp.zeros((16 - fp, hid), jnp.float32)
        wi_ref[...] = jnp.concatenate(
            [win_ref[...].astype(jnp.float32), rest], axis=0
        ).astype(half)
        rest = jnp.zeros((16 - outs, hid), jnp.float32)
        wo_ref[...] = jnp.concatenate(
            [wout_ref[...].astype(jnp.float32), rest], axis=0
        ).T.astype(half)
        accm[...] = jnp.zeros_like(accm)
        acci[...] = jnp.zeros_like(acci)
        acco[...] = jnp.zeros_like(acco)
        grads[...] = jnp.zeros_like(grads)

    def take_features():
        row = lax.broadcasted_iota(jnp.int32, (p.lines * 16, 128), 0)
        flat[...] = jnp.where((row % 16 >= fp) & (row % 16 < fp + 3), 1.0, 0.0)
        for f in range(fp):
            flat[pl.ds(f, p.lines, stride=16), :] = feat[f].astype(jnp.float32)
        for n in range(p.lines):
            sf_out[:, pl.ds(n * 128, 128)] = flat[pl.ds(n * 16, 16), :].astype(half)
        flat[...] = jnp.zeros_like(flat)

    if p.wide < 128:
        s1[...] = jnp.zeros_like(s1)
    moves1, moves2, moves3, moves4 = [], [], [], []
    for h in range(parts):
        stage1(h)
        if h == 0:
            pl.semaphore_wait(barrier, greeted)
        moves1.append(over_col(h, s1, d1, send1, recv1))
    take_weights()
    take_features()
    forward(1)
    for h in range(parts):
        arrived(moves1[h])
        stage2(h)
        moves2.append(over_row(h, s2, d2, send2, recv2))
        forward(3 + 3 * h)
    for h in range(parts):
        arrived(moves2[h])
    fields = stage3()
    for h in range(parts):
        stage4(h, fields)
        moves3.append(over_row(h, s3, d3, send3, recv3))
    forward(10)
    for h in range(parts):
        arrived(moves3[h])
        stage5(h)
        moves4.append(over_col(h, s4, d4, send4, recv4))
        forward(13 + 3 * h)
    forward(16)
    for i in range(max(0, steps - 2), steps):
        for copy in keep(i, i % 2):
            copy.wait()
    for i in range(min(steps, 2)):
        for copy in fetch(i, i):
            copy.start()
    for h in range(parts):
        arrived(moves4[h])
        stage6(h)
        lax.fori_loop(steps * h // parts, steps * (h + 1) // parts, backward_block, 0)
    width = hid // 2
    for side in range(2):
        part = slice(side * width, (side + 1) * width)
        grads[side, pl.ds(0, hid + 16), :] = accm[:, part]
        grads[side, pl.ds(hid + 16, 16), :] = acci[:, part]
        grads[side, pl.ds(hid + 32, 16), :] = acco[:, part]
    swap = pltpu.make_async_remote_copy(
        src_ref=grads.at[1 - core], dst_ref=pair, send_sem=send_a, recv_sem=recv_a,
        device_id=other, device_id_type=MESH,
    )
    swap.start()
    swap.wait_recv()
    held[...] = grads[core] + pair[...]
    spread, shared, handed = [], [], []
    for dz, dc in chips:
        z, c, device = chip(dz, dc)
        at = dz * cols + dc
        copy = pltpu.make_async_remote_copy(
            src_ref=held.at[place(z, c)], dst_ref=pieces.at[at], send_sem=send_b.at[at],
            recv_sem=recv_b.at[at], device_id=device, device_id_type=MESH,
        )
        copy.start()
        spread.append(copy)
    mine = place(me_z, me_c)
    value = held[mine, :]
    for copy, (dz, dc) in zip(spread, chips):
        copy.wait_recv()
        value = value + pieces[dz * cols + dc]
    total[mine, :] = value * factor

    def hand_over(at, where):
        copy = pltpu.make_async_remote_copy(
            src_ref=total.at[where], dst_ref=o_ref.at[core, where], send_sem=send_d.at[at],
            recv_sem=recv_d.at[at], device_id=other, device_id_type=MESH,
        )
        copy.start()
        handed.append(copy)

    for dz, dc in chips:
        at = dz * cols + dc
        copy = pltpu.make_async_remote_copy(
            src_ref=total.at[mine], dst_ref=total.at[mine], send_sem=send_c.at[at],
            recv_sem=recv_c.at[at], device_id=chip(dz, dc)[2], device_id_type=MESH,
        )
        copy.start()
        shared.append(copy)
    hand_over(0, mine)
    for copy, (dz, dc) in zip(shared, chips):
        copy.wait_recv()
        z, c, _ = chip(layers - dz, cols - dc)
        hand_over(dz * cols + dc, place(z, c))
    o_ref[core] = total[...]
    for copy in handed:
        copy.wait_recv()
    for copy in sends + [swap] + spread + shared + handed:
        copy.wait_send()


def whole(features, cotangent, w_in, bias_in, w_mid, bias_mid, w_out, rows, cols):
    p = Plan(cotangent.shape, rows, cols)
    feat, hid = w_in.shape
    cells = p.lines * p.nz
    block = math.gcd(cells, 4096)
    steps = cells // block
    count = rows // 2 * cols
    length = up(hid + 48, 8 * count)
    factor = 1.0 / math.sqrt(cells * rows * cols)
    dma = pltpu.SemaphoreType.DMA
    vmem = pl.BlockSpec(memory_space=pltpu.VMEM)
    hbm = pl.BlockSpec(memory_space=pl.ANY)
    single, half = jnp.float32, jnp.bfloat16
    parts = p.parts
    buffer = pltpu.VMEM((length, hid // 2), single)
    field, total, _, _ = pl.pallas_call(
        functools.partial(whole_kernel, p, feat, factor),
        out_shape=[
            jax.ShapeDtypeStruct((feat, p.lines, p.nz), single),
            jax.ShapeDtypeStruct((2, length, hid // 2), single),
            jax.ShapeDtypeStruct((steps, hid, block), half),
            jax.ShapeDtypeStruct((steps, hid, block), half),
        ],
        in_specs=[vmem] * 16,
        out_specs=[vmem, vmem, hbm, hbm],
        scratch_shapes=[
            pltpu.VMEM((parts, cols, p.rows1, 128), single),
            pltpu.VMEM((parts, cols, p.rows1, 128), single),
            pltpu.VMEM((parts, rows, p.rows2, 128), single),
            pltpu.VMEM((parts, rows, p.rows2, 128), single),
            pltpu.VMEM((parts, rows, p.rows3, 128), single),
            pltpu.VMEM((parts, rows, p.rows3, 128), single),
            pltpu.VMEM((parts, cols, p.rows4, 128), single),
            pltpu.VMEM((parts, cols, p.rows4, 128), single),
            pltpu.VMEM((2, p.kz * p.gp * p.xl, 128), single),
            pltpu.VMEM((p.kz * p.ns * p.hx, rows * 256), single),
            pltpu.VMEM((2, p.kz * p.ns * p.hx, 128), single),
            pltpu.VMEM((p.lines * 16, 128), single),
            pltpu.VMEM((2, hid + 16, block), half),
            pltpu.VMEM((2, hid, block), half),
            pltpu.VMEM((hid, 16), half),
            pltpu.VMEM((hid, hid), half),
            pltpu.VMEM((hid, 128), single),
            pltpu.VMEM((16, hid), half),
            pltpu.VMEM((hid, 16), half),
            pltpu.VMEM((16, cells), half),
            pltpu.VMEM((16, cells), half),
            pltpu.VMEM((hid + 16, hid), single),
            pltpu.VMEM((16, hid), single),
            pltpu.VMEM((16, hid), single),
            pltpu.VMEM((2, length, hid // 2), single),
            buffer,
            buffer,
            pltpu.VMEM((count, length // count, hid // 2), single),
            buffer,
            dma((parts, cols)), dma((parts, cols)), dma((parts, rows)), dma((parts, rows)),
            dma((parts, rows)), dma((parts, rows)), dma((parts, cols)), dma((parts, cols)),
            dma((2,)), dma((2,)), dma((2,)), dma((2,)),
            dma(()), dma(()), dma((count,)), dma((count,)), dma((count,)), dma((count,)),
            dma((count,)), dma((count,)),
        ],
        compiler_params=pltpu.CompilerParams(
            collective_id=1, has_side_effects=True, vmem_limit_bytes=58 << 20
        ),
        name="whole",
    )(
        cotangent.reshape(p.nc * p.lines, p.nz), features.reshape(feat, p.lines, p.nz),
        w_in, bias_in[None], w_mid, bias_mid[None], w_out.T, *p.tables(),
    )
    return field, total


def final_kernel(feat, outs, t_ref, win_ref, bin_ref, wmid_ref, bmid_ref, wout_ref):
    hid = wmid_ref.shape[0]
    side = hid // 2
    for n in range(2):
        lanes = pl.ds(n * side, side)
        wmid_ref[:, lanes] = t_ref[n, pl.ds(0, hid), :]
        bmid_ref[:, lanes] = t_ref[n, pl.ds(hid + feat, 1), :]
        win_ref[:, lanes] = t_ref[n, pl.ds(hid + 16, feat), :]
        bin_ref[:, lanes] = t_ref[n, pl.ds(hid + 16 + feat, 1), :]
        wout_ref[:, lanes] = t_ref[n, pl.ds(hid + 32, outs), :]


def final(total, feat, outs, hid):
    vmem = pl.BlockSpec(memory_space=pltpu.VMEM)
    single = jnp.float32
    return pl.pallas_call(
        functools.partial(final_kernel, feat, outs),
        out_shape=[
            jax.ShapeDtypeStruct((feat, hid), single),
            jax.ShapeDtypeStruct((1, hid), single),
            jax.ShapeDtypeStruct((hid, hid), single),
            jax.ShapeDtypeStruct((1, hid), single),
            jax.ShapeDtypeStruct((outs, hid), single),
        ],
        in_specs=[vmem],
        out_specs=[vmem] * 5,
        name="final",
    )(total)


def per_device(features, cotangent, w_in, bias_in, w_mid, bias_mid, w_out, rows, cols):
    field, total = whole(
        features, cotangent, w_in, bias_in, w_mid, bias_mid, w_out, rows, cols
    )
    g_in, b_in, g_mid, b_mid, g_out = final(total, features.shape[0], w_out.shape[1], len(w_mid))
    return field.reshape(features.shape), g_in, b_in[0], g_mid, b_mid[0], g_out.T


def solution(mesh):
    body = functools.partial(per_device, rows=mesh.shape["row"], cols=mesh.shape["col"])
    return jax.shard_map(
        body,
        mesh=mesh,
        in_specs=(
            P(None, None, "row", "col", None),
            P(None, None, "row", "col", None),
            P(),
            P(),
            P(),
            P(),
            P(),
        ),
        out_specs=(P(None, None, "row", "col", None), P(), P(), P(), P(), P()),
        check_vma=False,
    )
```

```python
import functools
import math

import jax
import jax.numpy as jnp
import numpy as np
from jax import lax
from jax.experimental import pallas as pl
from jax.experimental.pallas import tpu as pltpu
from jax.sharding import PartitionSpec as P

STEP_DT = 0.04
MESH = pl.DeviceIdType.MESH


def kept_modes(length):
    top = (length - 1) // 3
    return top


def padded(values, parts):
    share = -(-len(values) // parts)
    out = np.zeros((parts * share,), np.int64)
    out[: len(values)] = values
    live = np.zeros((parts * share,), np.float64)
    live[: len(values)] = 1.0
    return out.reshape(parts, share), live.reshape(parts, share)


def angles(modes, length):
    pos = np.arange(length)
    turns = (modes[..., None] * pos) % length
    return turns * (2.0 * math.pi / length)


def f32(a):
    return jnp.asarray(np.ascontiguousarray(a), jnp.float32)


def bf16(a):
    return jnp.asarray(np.ascontiguousarray(a), jnp.bfloat16)


def up(value, step):
    return step * (-(-value // step))


class Plan:
    def __init__(self, shape, rows, cols):
        self.nc, _, self.bx, self.by, self.nz = shape
        self.rows, self.cols = rows, cols
        self.nx, self.ny = self.bx * rows, self.by * cols
        self.mz, self.live_z = padded(np.arange(kept_modes(self.nz) + 1), cols)
        top_y, top_x = kept_modes(self.ny), kept_modes(self.nx)
        self.my, self.live_y = padded(np.arange(-top_y, top_y + 1), rows)
        self.mx = np.arange(-top_x, top_x + 1)
        self.kz, self.ky, self.kx = self.mz.shape[1], self.my.shape[1], len(self.mx)
        self.kxp = 8 * (-(-self.kx // 8))
        self.xl = max(d for d in range(1, self.bx + 1) if self.bx % d == 0 and d * self.by <= 128)
        self.xg = self.bx // self.xl
        self.wide = self.xl * self.by
        self.parts = 2 if self.xg % 2 == 0 and (self.bx // 2) % 8 == 0 else 1
        self.hg, self.hx = self.xg // self.parts, self.bx // self.parts
        self.gp = self.nc * self.hg
        while (self.kz * self.gp * self.xl) % 8:
            self.gp += 1
        self.modes = up(2 * self.kz, 8)
        self.rows1 = up(2 * self.kz * self.gp, 8)
        self.rows2 = self.nc * 2 * self.hx
        self.nf, self.ns = 4, 5
        self.rows3 = self.nf * 2 * self.hx
        self.sx = self.ns * self.hg
        self.rows4 = up(2 * self.kz * self.sx, 8)
        self.lines = self.bx * self.by

    def tables(self):
        kz, ky, kx, kxp = self.kz, self.ky, self.kx, self.kxp
        rows, cols, bx, by = self.rows, self.cols, self.bx, self.by
        az = angles(self.mz, self.nz)
        lz = self.live_z[..., None]
        t1 = np.zeros((cols, self.modes, self.nz))
        t1[:, :kz] = np.cos(az) * lz
        t1[:, kz : 2 * kz] = -np.sin(az) * lz
        weight = np.where(self.mz == 0, 1.0, 2.0)[..., None] * lz / self.nz
        t6 = np.zeros((cols, self.modes, self.nz))
        t6[:, :kz] = np.cos(az) * weight
        t6[:, kz : 2 * kz] = -np.sin(az) * weight
        ay = angles(self.my, self.ny)
        cy = np.cos(ay) * self.live_y[..., None]
        sy = np.sin(ay) * self.live_y[..., None]
        t2 = np.zeros((rows, 2, self.ny, 2, 128))
        t5 = np.zeros((rows, 2, 128, 2, self.ny))
        for k in range(ky):
            at = k * kz
            t2[:, 0, :, 0, at] = cy[:, k]
            t2[:, 1, :, 0, at] = sy[:, k]
            t2[:, 0, :, 1, at] = -sy[:, k]
            t2[:, 1, :, 1, at] = cy[:, k]
            t5[:, 0, at, 0] = cy[:, k] / self.ny
            t5[:, 1, at, 0] = -sy[:, k] / self.ny
            t5[:, 0, at, 1] = sy[:, k] / self.ny
            t5[:, 1, at, 1] = cy[:, k] / self.ny
        ax = angles(self.mx, self.nx)
        cx, sx = np.cos(ax), np.sin(ax)
        parts, hx = self.parts, self.hx
        t3 = np.zeros((2, kxp, rows, 2, bx))
        t4 = np.zeros((rows, 2, bx, 2, kxp))
        cr, sr = cx.reshape(kx, rows, bx), sx.reshape(kx, rows, bx)
        t3[0, :kx, :, 0] = cr
        t3[0, :kx, :, 1] = sr
        t3[1, :kx, :, 0] = -sr
        t3[1, :kx, :, 1] = cr
        scale = STEP_DT / self.nx
        ci, si = cr.transpose(1, 2, 0) * scale, sr.transpose(1, 2, 0) * scale
        t4[:, 0, :, 0, :kx] = -si
        t4[:, 0, :, 1, :kx] = -ci
        t4[:, 1, :, 0, :kx] = ci
        t4[:, 1, :, 1, :kx] = -si
        t3 = t3.reshape(2, kxp, rows, 2, parts, hx).transpose(0, 1, 4, 2, 3, 5)
        t4 = t4.reshape(rows, 2, parts, hx, 2, kxp).transpose(2, 0, 1, 3, 4, 5)
        lane_y = np.zeros((rows, 1, 128))
        lane_z = np.zeros((cols, 1, 128))
        lane_y[:, 0, : ky * kz] = np.repeat(self.my, kz, axis=1)
        lane_z[:, 0, : ky * kz] = np.tile(self.mz, (1, ky))
        wave_x = np.zeros((kxp, 128))
        wave_x[:kx] = self.mx[:, None]
        return (
            bf16(t1.reshape(cols * self.modes, self.nz)),
            bf16(t2.reshape(rows, 2 * self.ny, 256)),
            bf16(t3.reshape(2 * kxp, rows * 2 * bx)),
            bf16(t4.reshape(parts, rows * 2 * hx, 2 * kxp)),
            bf16(t5.reshape(rows * 256, 2 * self.ny)),
            bf16(t6.reshape(cols * self.modes, self.nz)),
            f32(wave_x),
            f32(lane_y),
            f32(lane_z),
        )


def whole_kernel(p, fp, factor, cot, feat, win_ref, bin_ref, wmid_ref, bmid_ref, wout_ref,
                    t1, t2, t3, t4, t5, t6, wx_ref, wy_ref, wz_ref,
                    field, o_ref, r_ref, act_in, act_mid,
                    s1, d1, s2, d2, s3, d3, s4, d4, e2, q5, o5, flat, abuf, mbuf,
                    w1_ref, w2_ref, b2_ref, wi_ref, wo_ref, sf_out, sg_out, accm, acci, acco,
                    grads, pair, held, pieces, total, later, gbuf, rest, rest_p, rest_c, rest_z,
                    send1, recv1, send2, recv2, send3, recv3, send4, recv4, sem_a, sem_m,
                    load_a, load_m, send_a, recv_a, send_b, recv_b, send_c, recv_c,
                    send_d, recv_d, send_e, recv_e, send_f, recv_f, send_g, recv_g, sem_g):
    me_r, me_c = lax.axis_index("row"), lax.axis_index("col")
    rows, cols, kz, ky, kxp = p.rows, p.cols, p.kz, p.ky, p.kxp
    bx, by, nc, hx, parts = p.bx, p.by, p.nc, p.hx, p.parts
    last = (((1,), (1,)), ((), ()))
    first = (((0,), (0,)), ((), ()))
    half = jnp.bfloat16

    def row_peer(d):
        return lax.rem(me_r + d, rows)

    def col_peer(d):
        return lax.rem(me_c + d, cols)

    barrier = pltpu.get_barrier_semaphore()
    for d in range(1, rows):
        pl.semaphore_signal(barrier, inc=1, device_id=(row_peer(d), me_c), device_id_type=MESH)
    for d in range(1, cols):
        pl.semaphore_signal(barrier, inc=1, device_id=(me_r, col_peer(d)), device_id_type=MESH)
    layers = rows // 2
    core, me_z = lax.rem(me_r, 2), me_r // 2
    other = (me_r + 1 - 2 * core, me_c)
    share = pieces.shape[1]

    def chip(dz, dc):
        z, c = lax.rem(me_z + dz, layers), lax.rem(me_c + dc, cols)
        return z, c, (2 * z + core, c)

    def place(z, c):
        return pl.ds(pl.multiple_of((z * cols + c) * share, 8), share)

    chips = [(dz, dc) for dz in range(layers) for dc in range(cols) if dz or dc]
    greeted = rows + cols - 2
    for dz, dc in chips:
        if dz and dc:
            greeted += 1
            pl.semaphore_signal(barrier, inc=1, device_id=chip(dz, dc)[2], device_id_type=MESH)
    sends = []

    def over_col(h, src, dst, send, recv):
        copies = []
        for d in range(1, cols):
            copy = pltpu.make_async_remote_copy(
                src_ref=src.at[h, col_peer(d)], dst_ref=dst.at[h, me_c], send_sem=send.at[h, d],
                recv_sem=recv.at[h, d], device_id=(me_r, col_peer(d)), device_id_type=MESH,
            )
            copy.start()
            copies.append(copy)
        dst[h, me_c] = src[h, me_c]
        sends.extend(copies)
        return copies

    def over_row(h, src, dst, send, recv):
        copies = []
        for d in range(1, rows):
            copy = pltpu.make_async_remote_copy(
                src_ref=src.at[h, row_peer(d)], dst_ref=dst.at[h, me_r], send_sem=send.at[h, d],
                recv_sem=recv.at[h, d], device_id=(row_peer(d), me_c), device_id_type=MESH,
            )
            copy.start()
            copies.append(copy)
        dst[h, me_r] = src[h, me_r]
        sends.extend(copies)
        return copies

    def arrived(copies):
        for copy in copies:
            copy.wait_recv()

    steps, hid, block = act_in.shape
    inner = math.gcd(block, 512)
    done = [0]

    def keep(i, slot):
        return (
            pltpu.make_async_copy(
                abuf.at[slot, pl.ds(0, hid)], act_in.at[i], sem_a.at[slot]
            ),
            pltpu.make_async_copy(mbuf.at[slot], act_mid.at[i], sem_m.at[slot]),
        )

    def forward_block(i, carry):
        slot = lax.rem(i, 2)

        @pl.when(i >= 2)
        def _():
            for copy in keep(i, slot):
                copy.wait()

        src = sf_out[:, pl.ds(pl.multiple_of(i * block, block), block)]
        pre = jnp.dot(w1_ref[...], src, preferred_element_type=jnp.float32)
        act = jnp.tanh(pre).astype(half)
        abuf[slot, pl.ds(0, hid), :] = act
        pre = jnp.dot(w2_ref[...], act, preferred_element_type=jnp.float32) + b2_ref[:, :1]
        mbuf[slot] = jnp.tanh(pre).astype(half)
        for copy in keep(i, slot):
            copy.start()
        return carry

    def fetch(i, slot):
        return (
            pltpu.make_async_copy(
                act_in.at[i], abuf.at[slot, pl.ds(0, hid)], load_a.at[slot]
            ),
            pltpu.make_async_copy(act_mid.at[i], mbuf.at[slot], load_m.at[slot]),
        )

    later_from = steps // parts if parts > 1 else steps
    wide_inner = math.gcd(block, 2048)

    def put(i, slot):
        return pltpu.make_async_copy(
            gbuf.at[slot], field.at[:, pl.ds(i * (block // 128), block // 128), :], sem_g.at[slot]
        )

    def before_put(i, slot):
        @pl.when(i >= 2)
        def _():
            put(i, slot).wait()

    def finish(i, slot, first_lane, delta, size):
        start = pl.multiple_of(i * block + first_lane, size)
        acci[...] += lax.dot_general(
            sf_out[:, pl.ds(start, size)], delta, last, preferred_element_type=jnp.float32
        )
        grad = jnp.dot(wi_ref[...], delta, preferred_element_type=jnp.float32)
        for row in range(size // 128):
            gbuf[slot, :, first_lane // 128 + row, :] = grad[:fp, row * 128 : (row + 1) * 128]

    def later_block(k, carry):
        i = k + later_from
        slot = lax.rem(i, 2)
        before_put(i, slot)
        for n in range(block // wide_inner):
            delta = later[k, :, pl.ds(n * wide_inner, wide_inner)]
            finish(i, slot, n * wide_inner, delta, wide_inner)
        put(i, slot).start()
        return carry

    def backward_block(defer, i, carry):
        slot = lax.rem(i, 2)
        if not defer:
            before_put(i, slot)
        for copy in fetch(i, slot):
            copy.wait()
        start = pl.multiple_of(i * block, block)
        abuf[slot, pl.ds(hid, 16), :] = sf_out[:, pl.ds(start, block)]
        back_mid, delta_mid, back_in, delta_in = {}, {}, {}, {}

        def lanes(n):
            return pl.ds(n * inner, inner)

        def source(ref, n):
            return ref[:, pl.ds(pl.multiple_of(start + n * inner, inner), inner)]

        def gate(back, act):
            wide = act.astype(jnp.float32)
            return (back * (1.0 - wide * wide)).astype(half)

        def enter(n):
            sg, act = source(sg_out, n), mbuf[slot, :, lanes(n)]
            acco[...] += lax.dot_general(sg, act, last, preferred_element_type=jnp.float32)
            back_mid[n] = jnp.dot(wo_ref[...], sg, preferred_element_type=jnp.float32)

        def middle(n):
            delta_mid[n] = gate(back_mid.pop(n), mbuf[slot, :, lanes(n)])

        def weigh(n):
            delta = delta_mid.pop(n)
            back_in[n] = jnp.dot(wmid_ref[...], delta, preferred_element_type=jnp.float32)
            accm[...] += lax.dot_general(
                abuf[slot, :, lanes(n)], delta, last, preferred_element_type=jnp.float32
            )

        def lower(n):
            delta_in[n] = gate(back_in.pop(n), abuf[slot, pl.ds(0, hid), lanes(n)])

        def leave(n):
            delta = delta_in.pop(n)
            if defer:
                later[i - later_from, :, lanes(n)] = delta
            else:
                finish(i, slot, n * inner, delta, inner)

        count = block // inner
        for turn in range(count + 4):
            for late, work in ((4, leave), (3, lower), (2, weigh), (1, middle), (0, enter)):
                if 0 <= turn - late < count:
                    work(turn - late)
        if not defer:
            put(i, slot).start()

        @pl.when(i + 2 < steps)
        def _():
            for copy in fetch(i + 2, slot):
                copy.start()

        return carry

    def forward(share):
        upto = min(steps, -(-steps * share // 16))
        if upto > done[0]:
            lax.fori_loop(done[0], upto, forward_block, 0)
            done[0] = upto

    def stage1(h):
        for v in range(nc):
            for g in range(p.hg):
                at = v * p.xg + h * p.hg + g
                a = cot[pl.ds(at * p.wide, p.wide), :].astype(half)
                part = lax.dot_general(t1[...], a, last, preferred_element_type=jnp.float32)
                for c in range(cols):
                    s1[h, c, pl.ds(v * p.hg + g, 2 * kz, stride=p.gp), pl.ds(0, p.wide)] = part[
                        c * p.modes : c * p.modes + 2 * kz
                    ]

    def stage2(h):
        count = kz * p.gp
        where = lax.broadcasted_iota(jnp.int32, (count, 128), 1) // by
        for ri in range(2):
            for j in range(p.xl):
                whole = None
                for c in range(cols):
                    tile = d1[h, c, pl.ds(ri * count, count), :]
                    shift = ((c - j) * by) % 128
                    tile = tile if shift == 0 else pltpu.roll(tile, shift, 1)
                    whole = tile if whole is None else jnp.where(where == c, tile, whole)
                e2[ri, pl.ds(j, count, stride=p.xl), :] = whole
        lhs = jnp.concatenate([e2[0].astype(half), e2[1].astype(half)], axis=1)
        per = p.gp * p.xl
        for r in range(rows):
            part = jnp.dot(lhs, t2[r], preferred_element_type=jnp.float32)
            for ri in range(2):
                total = part[:per, ri * 128 : (ri + 1) * 128]
                for k in range(1, kz):
                    total = total + pltpu.roll(
                        part[k * per : (k + 1) * per, ri * 128 : (ri + 1) * 128], k, 1
                    )
                for v in range(nc):
                    s2[h, r, pl.ds((2 * v + ri) * hx, hx), :] = total[v * hx : (v + 1) * hx]

    def stage3():
        wx, wy, wz = wx_ref[...], wy_ref[me_r], wz_ref[me_c]
        vel = []
        for v in range(nc):
            data = jnp.concatenate(
                [d2[h, r, pl.ds(2 * v * hx, 2 * hx), :] for h in range(parts) for r in range(rows)],
                axis=0,
            )
            hat = jnp.dot(t3[...], data.astype(half), preferred_element_type=jnp.float32)
            vel.append((hat[:kxp], hat[kxp:]))
        inverse = 1.0 / jnp.maximum(wx * wx + wy * wy + wz * wz, 1.0)
        fields = [[], [], [], []]
        for ri in range(2):
            inner = (wx * vel[0][ri] + wy * vel[1][ri] + wz * vel[2][ri]) * inverse
            px = vel[0][ri] - wx * inner
            py = vel[1][ri] - wy * inner
            pz = vel[2][ri] - wz * inner
            fields[0].append(py)
            fields[1].append(pz)
            fields[2].append(wy * px + wx * py)
            fields[3].append(wz * px + wx * pz)
        return [jnp.concatenate(field, axis=0).astype(half) for field in fields]

    def stage4(h, fields):
        for f in range(p.nf):
            part = jnp.dot(t4[h], fields[f], preferred_element_type=jnp.float32)
            for r in range(rows):
                s3[h, r, pl.ds(f * 2 * hx, 2 * hx), :] = part[r * 2 * hx : (r + 1) * 2 * hx]

    def stage5(h):
        span = p.ns * hx
        for r in range(rows):
            wy, wz = wy_ref[r], wz_ref[me_c]
            for ri in range(2):
                qy, qz, xy, xz = [d3[h, r, pl.ds((2 * f + ri) * hx, hx), :] for f in range(p.nf)]
                data = jnp.concatenate([wy * qy, wz * qz, xy, xz, wz * qy + wy * qz], axis=0)
                for k in range(kz):
                    tile = data if k == 0 else pltpu.roll(data, 128 - k, 1)
                    q5[pl.ds(k * span, span), pl.ds((2 * r + ri) * 128, 128)] = tile
        part = jnp.dot(q5[...].astype(half), t5[...], preferred_element_type=jnp.float32)
        for ri in range(2):
            o5[ri] = part[:, ri * 128 : (ri + 1) * 128]
        count = kz * p.sx
        where = lax.broadcasted_iota(jnp.int32, (count, 128), 1) // by
        for ri in range(2):
            tiles = [o5[ri, pl.ds(j, count, stride=p.xl), :] for j in range(p.xl)]
            for c in range(cols):
                whole = None
                for j in range(p.xl):
                    shift = ((j - c) * by) % 128
                    tile = tiles[j] if shift == 0 else pltpu.roll(tiles[j], shift, 1)
                    whole = tile if whole is None else jnp.where(where == j, tile, whole)
                s4[h, c, pl.ds(ri * count, count), :] = whole

    def stage6(h):
        pad = jnp.zeros((p.modes - 2 * kz, 128), jnp.float32)
        for g in range(p.hg):
            comps = []
            for comp in range(p.ns):
                pieces = []
                for c in range(cols):
                    pieces.append(d4[h, c, pl.ds(comp * p.hg + g, 2 * kz, stride=p.sx), :])
                    if p.modes > 2 * kz:
                        pieces.append(pad)
                data = jnp.concatenate(pieces, axis=0).astype(half)
                comps.append(
                    lax.dot_general(data, t6[...], first, preferred_element_type=jnp.float32)[
                        : p.wide
                    ]
                )
            order = [-(comps[0] + comps[1]), comps[0], comps[1], comps[2], comps[3], comps[4]]
            line = (h * p.hg + g) * p.wide
            for comp in range(6):
                flat[pl.ds(line * 16 + comp, p.wide, stride=16), :] = order[comp]
            for n in range(p.wide):
                sg_out[:, pl.ds((line + n) * 128, 128)] = flat[
                    pl.ds((line + n) * 16, 16), :
                ].astype(half)

    def take_weights():
        bias = bin_ref[...]
        high = bias.astype(half).astype(jnp.float32)
        middle = (bias - high).astype(half).astype(jnp.float32)
        low = bias - high - middle
        blank = jnp.zeros((16 - fp - 3, hid), jnp.float32)
        table = jnp.concatenate(
            [win_ref[...].astype(jnp.float32), high, middle, low, blank], axis=0
        )
        w1_ref[...] = table.T.astype(half)
        w2_ref[...] = wmid_ref[...].astype(jnp.float32).T.astype(half)
        b2_ref[...] = jnp.broadcast_to(bmid_ref[...], (128, hid)).T
        outs = wout_ref.shape[0]
        blank = jnp.zeros((16 - fp, hid), jnp.float32)
        wi_ref[...] = jnp.concatenate(
            [win_ref[...].astype(jnp.float32), blank], axis=0
        ).astype(half)
        blank = jnp.zeros((16 - outs, hid), jnp.float32)
        wo_ref[...] = jnp.concatenate(
            [wout_ref[...].astype(jnp.float32), blank], axis=0
        ).T.astype(half)
        accm[...] = jnp.zeros_like(accm)
        acci[...] = jnp.zeros_like(acci)
        acco[...] = jnp.zeros_like(acco)
        if grads.shape[1] > hid:
            grads[...] = jnp.zeros_like(grads)
        rest[...] = jnp.zeros_like(rest)

    def take_features():
        for f in range(16):
            if f < fp:
                value = feat[f].astype(jnp.float32)
            else:
                value = jnp.full((p.lines, 128), 1.0 if f < fp + 3 else 0.0, jnp.float32)
            flat[pl.ds(f, p.lines, stride=16), :] = value
        for n in range(p.lines):
            sf_out[:, pl.ds(n * 128, 128)] = flat[pl.ds(n * 16, 16), :].astype(half)

    if p.wide < 128:
        s1[...] = jnp.zeros_like(s1)
    moves1, moves2, moves3, moves4 = [], [], [], []
    for h in range(parts):
        stage1(h)
        if h == 0:
            pl.semaphore_wait(barrier, greeted)
        moves1.append(over_col(h, s1, d1, send1, recv1))
    take_features()
    for h in range(parts):
        arrived(moves1[h])
        stage2(h)
        moves2.append(over_row(h, s2, d2, send2, recv2))
        if h == 0:
            take_weights()
    forward(5)
    for h in range(parts):
        arrived(moves2[h])
    fields = stage3()
    for h in range(parts):
        stage4(h, fields)
        moves3.append(over_row(h, s3, d3, send3, recv3))
        forward(8 + 2 * h)
    for h in range(parts):
        arrived(moves3[h])
        stage5(h)
        moves4.append(over_col(h, s4, d4, send4, recv4))
        forward(13 + 3 * h)
    forward(16)
    for i in range(max(0, steps - 2), steps):
        for copy in keep(i, i % 2):
            copy.wait()
    for i in range(min(steps, 2)):
        for copy in fetch(i, i):
            copy.start()
    for h in range(parts):
        arrived(moves4[h])
        stage6(h)
        lax.fori_loop(
            steps * h // parts, steps * (h + 1) // parts,
            functools.partial(backward_block, h > 0), 0,
        )
    width = hid // 2
    for side in range(2):
        grads[side, pl.ds(0, hid), :] = accm[pl.ds(0, hid), side * width : (side + 1) * width]
    swap = pltpu.make_async_remote_copy(
        src_ref=grads.at[1 - core], dst_ref=pair, send_sem=send_a, recv_sem=recv_a,
        device_id=other, device_id_type=MESH,
    )
    swap.start()
    left = steps - later_from
    lax.fori_loop(0, left // 8, later_block, 0)
    swap.wait_recv()
    held[...] = grads[core] + pair[...]
    spread, shared, handed, small = [], [], [], []
    for dz, dc in chips:
        z, c, device = chip(dz, dc)
        at = dz * cols + dc
        copy = pltpu.make_async_remote_copy(
            src_ref=held.at[place(z, c)], dst_ref=pieces.at[at], send_sem=send_b.at[at],
            recv_sem=recv_b.at[at], device_id=device, device_id_type=MESH,
        )
        copy.start()
        spread.append(copy)
    lax.fori_loop(left // 8, left, later_block, 0)
    outs = wout_ref.shape[0]
    rest[pl.ds(0, fp + 1), :] = acci[pl.ds(0, fp + 1), :]
    rest[pl.ds(fp + 1, outs), :] = acco[pl.ds(0, outs), :]
    rest[pl.ds(fp + 1 + outs, 1), :] = accm[pl.ds(hid + fp, 1), :]
    trade = pltpu.make_async_remote_copy(
        src_ref=rest, dst_ref=rest_p, send_sem=send_e, recv_sem=recv_e,
        device_id=other, device_id_type=MESH,
    )
    trade.start()
    small.append(trade)
    mine = place(me_z, me_c)
    value = held[mine, :]
    for copy, (dz, dc) in zip(spread, chips):
        copy.wait_recv()
        value = value + pieces[dz * cols + dc]
    total[mine, :] = value * factor

    def hand_over(at, where):
        copy = pltpu.make_async_remote_copy(
            src_ref=total.at[where], dst_ref=o_ref.at[core, where], send_sem=send_d.at[at],
            recv_sem=recv_d.at[at], device_id=other, device_id_type=MESH,
        )
        copy.start()
        handed.append(copy)

    trade.wait_recv()
    rest_c[me_c] = rest[...] + rest_p[...]
    moves = []
    for dc in range(1, cols):
        copy = pltpu.make_async_remote_copy(
            src_ref=rest_c.at[me_c], dst_ref=rest_c.at[me_c], send_sem=send_f.at[dc],
            recv_sem=recv_f.at[dc], device_id=(me_r, col_peer(dc)), device_id_type=MESH,
        )
        copy.start()
        moves.append(copy)
    small.extend(moves)
    for dz, dc in chips:
        at = dz * cols + dc
        copy = pltpu.make_async_remote_copy(
            src_ref=total.at[mine], dst_ref=total.at[mine], send_sem=send_c.at[at],
            recv_sem=recv_c.at[at], device_id=chip(dz, dc)[2], device_id_type=MESH,
        )
        copy.start()
        shared.append(copy)
    hand_over(0, mine)
    arrived(moves)
    value = rest_c[0]
    for c in range(1, cols):
        value = value + rest_c[c]
    rest_z[me_z] = value
    moves = []
    for dz in range(1, layers):
        copy = pltpu.make_async_remote_copy(
            src_ref=rest_z.at[me_z], dst_ref=rest_z.at[me_z], send_sem=send_g.at[dz],
            recv_sem=recv_g.at[dz], device_id=chip(dz, 0)[2], device_id_type=MESH,
        )
        copy.start()
        moves.append(copy)
    small.extend(moves)
    for copy, (dz, dc) in zip(shared, chips):
        copy.wait_recv()
        z, c, _ = chip(layers - dz, cols - dc)
        hand_over(dz * cols + dc, place(z, c))
    arrived(moves)
    value = rest_z[0]
    for z in range(1, layers):
        value = value + rest_z[z]
    r_ref[...] = value * factor
    o_ref[core] = total[...]
    arrived(handed)
    for i in range(max(0, steps - 2), steps):
        put(i, i % 2).wait()
    for copy in sends + [swap] + spread + shared + handed + small:
        copy.wait_send()


def whole(features, cotangent, w_in, bias_in, w_mid, bias_mid, w_out, rows, cols):
    p = Plan(cotangent.shape, rows, cols)
    feat, hid = w_in.shape
    cells = p.lines * p.nz
    block = math.gcd(cells, 4096)
    steps = cells // block
    count = rows // 2 * cols
    length = up(hid, 8 * count)
    few = up(feat + 2 + w_out.shape[1], 8)
    layers = rows // 2
    factor = 1.0 / math.sqrt(cells * rows * cols)
    dma = pltpu.SemaphoreType.DMA
    vmem = pl.BlockSpec(memory_space=pltpu.VMEM)
    hbm = pl.BlockSpec(memory_space=pl.ANY)
    single, half = jnp.float32, jnp.bfloat16
    parts = p.parts
    buffer = pltpu.VMEM((length, hid // 2), single)
    field, total, rest, _, _ = pl.pallas_call(
        functools.partial(whole_kernel, p, feat, factor),
        out_shape=[
            jax.ShapeDtypeStruct((feat, p.lines, p.nz), single),
            jax.ShapeDtypeStruct((2, length, hid // 2), single),
            jax.ShapeDtypeStruct((few, hid), single),
            jax.ShapeDtypeStruct((steps, hid, block), half),
            jax.ShapeDtypeStruct((steps, hid, block), half),
        ],
        in_specs=[vmem] * 16,
        out_specs=[hbm, vmem, vmem, hbm, hbm],
        scratch_shapes=[
            pltpu.VMEM((parts, cols, p.rows1, 128), single),
            pltpu.VMEM((parts, cols, p.rows1, 128), single),
            pltpu.VMEM((parts, rows, p.rows2, 128), single),
            pltpu.VMEM((parts, rows, p.rows2, 128), single),
            pltpu.VMEM((parts, rows, p.rows3, 128), single),
            pltpu.VMEM((parts, rows, p.rows3, 128), single),
            pltpu.VMEM((parts, cols, p.rows4, 128), single),
            pltpu.VMEM((parts, cols, p.rows4, 128), single),
            pltpu.VMEM((2, p.kz * p.gp * p.xl, 128), single),
            pltpu.VMEM((p.kz * p.ns * p.hx, rows * 256), single),
            pltpu.VMEM((2, p.kz * p.ns * p.hx, 128), single),
            pltpu.VMEM((p.lines * 16, 128), single),
            pltpu.VMEM((2, hid + 16, block), half),
            pltpu.VMEM((2, hid, block), half),
            pltpu.VMEM((hid, 16), half),
            pltpu.VMEM((hid, hid), half),
            pltpu.VMEM((hid, 128), single),
            pltpu.VMEM((16, hid), half),
            pltpu.VMEM((hid, 16), half),
            pltpu.VMEM((16, cells), half),
            pltpu.VMEM((16, cells), half),
            pltpu.VMEM((hid + 16, hid), single),
            pltpu.VMEM((16, hid), single),
            pltpu.VMEM((16, hid), single),
            pltpu.VMEM((2, length, hid // 2), single),
            buffer,
            buffer,
            pltpu.VMEM((count, length // count, hid // 2), single),
            buffer,
            pltpu.VMEM((max(1, steps - steps // parts), hid, block), half),
            pltpu.VMEM((2, feat, block // 128, 128), single),
            pltpu.VMEM((few, hid), single),
            pltpu.VMEM((few, hid), single),
            pltpu.VMEM((cols, few, hid), single),
            pltpu.VMEM((layers, few, hid), single),
            dma((parts, cols)), dma((parts, cols)), dma((parts, rows)), dma((parts, rows)),
            dma((parts, rows)), dma((parts, rows)), dma((parts, cols)), dma((parts, cols)),
            dma((2,)), dma((2,)), dma((2,)), dma((2,)),
            dma(()), dma(()), dma((count,)), dma((count,)), dma((count,)), dma((count,)),
            dma((count,)), dma((count,)),
            dma(()), dma(()), dma((cols,)), dma((cols,)), dma((layers,)), dma((layers,)), dma((2,)),
        ],
        compiler_params=pltpu.CompilerParams(
            collective_id=1, has_side_effects=True, vmem_limit_bytes=58 << 20
        ),
        name="whole",
    )(
        cotangent.reshape(p.nc * p.lines, p.nz), features.reshape(feat, p.lines, p.nz),
        w_in, bias_in[None], w_mid, bias_mid[None], w_out.T, *p.tables(),
    )
    return field, total, rest


def final_kernel(feat, outs, f_ref, t_ref, r_ref,
                 field_ref, win_ref, bin_ref, wmid_ref, bmid_ref, wout_ref,
                 held, into, away):
    arrive = [pltpu.make_async_copy(f_ref.at[f], held.at[f], into.at[f]) for f in range(feat)]
    depart = [pltpu.make_async_copy(held.at[f], field_ref.at[f], away.at[f]) for f in range(feat)]
    for copy in arrive:
        copy.start()
    hid = wmid_ref.shape[0]
    side = hid // 2
    for n in range(2):
        wmid_ref[:, pl.ds(n * side, side)] = t_ref[n, pl.ds(0, hid), :]
    win_ref[...] = r_ref[pl.ds(0, feat), :]
    bin_ref[...] = r_ref[pl.ds(feat, 1), :]
    wout_ref[...] = r_ref[pl.ds(feat + 1, outs), :]
    bmid_ref[...] = r_ref[pl.ds(feat + 1 + outs, 1), :]
    for coming, going in zip(arrive, depart):
        coming.wait()
        going.start()
    for copy in depart:
        copy.wait()


def final(field, total, rest, feat, outs, hid):
    vmem = pl.BlockSpec(memory_space=pltpu.VMEM)
    hbm = pl.BlockSpec(memory_space=pl.ANY)
    single = jnp.float32
    return pl.pallas_call(
        functools.partial(final_kernel, feat, outs),
        out_shape=[
            jax.ShapeDtypeStruct(field.shape, single),
            jax.ShapeDtypeStruct((feat, hid), single),
            jax.ShapeDtypeStruct((1, hid), single),
            jax.ShapeDtypeStruct((hid, hid), single),
            jax.ShapeDtypeStruct((1, hid), single),
            jax.ShapeDtypeStruct((outs, hid), single),
        ],
        in_specs=[hbm, vmem, vmem],
        out_specs=[hbm] + [vmem] * 5,
        scratch_shapes=[
            pltpu.VMEM(field.shape, single),
            pltpu.SemaphoreType.DMA((feat,)),
            pltpu.SemaphoreType.DMA((feat,)),
        ],
        name="final",
    )(field, total, rest)


def per_device(features, cotangent, w_in, bias_in, w_mid, bias_mid, w_out, rows, cols):
    field, total, rest = whole(
        features, cotangent, w_in, bias_in, w_mid, bias_mid, w_out, rows, cols
    )
    field, g_in, b_in, g_mid, b_mid, g_out = final(
        field, total, rest, features.shape[0], w_out.shape[1], len(w_mid)
    )
    return field.reshape(features.shape), g_in, b_in[0], g_mid, b_mid[0], g_out.T


def solution(mesh):
    body = functools.partial(per_device, rows=mesh.shape["row"], cols=mesh.shape["col"])
    return jax.shard_map(
        body,
        mesh=mesh,
        in_specs=(
            P(None, None, "row", "col", None),
            P(None, None, "row", "col", None),
            P(),
            P(),
            P(),
            P(),
            P(),
        ),
        out_specs=(P(None, None, "row", "col", None), P(), P(), P(), P(), P()),
        check_vma=False,
    )
```

```python
import functools
import math

import jax
import jax.numpy as jnp
import numpy as np
from jax import lax
from jax.experimental import pallas as pl
from jax.experimental.pallas import tpu as pltpu
from jax.sharding import PartitionSpec as P

STEP_DT = 0.04
MESH = pl.DeviceIdType.MESH


def kept_modes(length):
    top = (length - 1) // 3
    return top


def padded(values, parts):
    share = -(-len(values) // parts)
    out = np.zeros((parts * share,), np.int64)
    out[: len(values)] = values
    live = np.zeros((parts * share,), np.float64)
    live[: len(values)] = 1.0
    return out.reshape(parts, share), live.reshape(parts, share)


def angles(modes, length):
    pos = np.arange(length)
    turns = (modes[..., None] * pos) % length
    return turns * (2.0 * math.pi / length)


def f32(a):
    return jnp.asarray(np.ascontiguousarray(a), jnp.float32)


def bf16(a):
    return jnp.asarray(np.ascontiguousarray(a), jnp.bfloat16)


def up(value, step):
    return step * (-(-value // step))


class Plan:
    def __init__(self, shape, rows, cols):
        self.nc, _, self.bx, self.by, self.nz = shape
        self.rows, self.cols = rows, cols
        self.nx, self.ny = self.bx * rows, self.by * cols
        self.mz, self.live_z = padded(np.arange(kept_modes(self.nz) + 1), cols)
        top_y, top_x = kept_modes(self.ny), kept_modes(self.nx)
        self.my, self.live_y = padded(np.arange(-top_y, top_y + 1), rows)
        self.mx = np.arange(-top_x, top_x + 1)
        self.kz, self.ky, self.kx = self.mz.shape[1], self.my.shape[1], len(self.mx)
        self.kxp = 8 * (-(-self.kx // 8))
        self.xl = max(d for d in range(1, self.bx + 1) if self.bx % d == 0 and d * self.by <= 128)
        self.xg = self.bx // self.xl
        self.wide = self.xl * self.by
        self.parts = 2 if self.xg % 2 == 0 and (self.bx // 2) % 8 == 0 else 1
        self.hg, self.hx = self.xg // self.parts, self.bx // self.parts
        self.gp = self.nc * self.hg
        while (self.kz * self.gp * self.xl) % 8:
            self.gp += 1
        self.modes = up(2 * self.kz, 8)
        self.rows1 = up(2 * self.kz * self.gp, 8)
        self.rows2 = self.nc * 2 * self.hx
        self.nf, self.ns = 4, 5
        self.rows3 = self.nf * 2 * self.hx
        self.sx = self.ns * self.hg
        self.rows4 = up(2 * self.kz * self.sx, 8)
        self.lines = self.bx * self.by

    def tables(self):
        kz, ky, kx, kxp = self.kz, self.ky, self.kx, self.kxp
        rows, cols, bx, by = self.rows, self.cols, self.bx, self.by
        az = angles(self.mz, self.nz)
        lz = self.live_z[..., None]
        t1 = np.zeros((cols, self.modes, self.nz))
        t1[:, :kz] = np.cos(az) * lz
        t1[:, kz : 2 * kz] = -np.sin(az) * lz
        weight = np.where(self.mz == 0, 1.0, 2.0)[..., None] * lz / self.nz
        t6 = np.zeros((cols, self.modes, self.nz))
        t6[:, :kz] = np.cos(az) * weight
        t6[:, kz : 2 * kz] = -np.sin(az) * weight
        ay = angles(self.my, self.ny)
        cy = np.cos(ay) * self.live_y[..., None]
        sy = np.sin(ay) * self.live_y[..., None]
        t2 = np.zeros((rows, 2, self.ny, 2, 128))
        t5 = np.zeros((rows, 2, 128, 2, self.ny))
        for k in range(ky):
            at = k * kz
            t2[:, 0, :, 0, at] = cy[:, k]
            t2[:, 1, :, 0, at] = sy[:, k]
            t2[:, 0, :, 1, at] = -sy[:, k]
            t2[:, 1, :, 1, at] = cy[:, k]
            t5[:, 0, at, 0] = cy[:, k] / self.ny
            t5[:, 1, at, 0] = -sy[:, k] / self.ny
            t5[:, 0, at, 1] = sy[:, k] / self.ny
            t5[:, 1, at, 1] = cy[:, k] / self.ny
        ax = angles(self.mx, self.nx)
        cx, sx = np.cos(ax), np.sin(ax)
        parts, hx = self.parts, self.hx
        t3 = np.zeros((2, kxp, rows, 2, bx))
        t4 = np.zeros((rows, 2, bx, 2, kxp))
        cr, sr = cx.reshape(kx, rows, bx), sx.reshape(kx, rows, bx)
        t3[0, :kx, :, 0] = cr
        t3[0, :kx, :, 1] = sr
        t3[1, :kx, :, 0] = -sr
        t3[1, :kx, :, 1] = cr
        scale = STEP_DT / self.nx
        ci, si = cr.transpose(1, 2, 0) * scale, sr.transpose(1, 2, 0) * scale
        t4[:, 0, :, 0, :kx] = -si
        t4[:, 0, :, 1, :kx] = -ci
        t4[:, 1, :, 0, :kx] = ci
        t4[:, 1, :, 1, :kx] = -si
        t3 = t3.reshape(2, kxp, rows, 2, parts, hx).transpose(0, 1, 4, 2, 3, 5)
        t4 = t4.reshape(rows, 2, parts, hx, 2, kxp).transpose(2, 0, 1, 3, 4, 5)
        lane_y = np.zeros((rows, 1, 128))
        lane_z = np.zeros((cols, 1, 128))
        lane_y[:, 0, : ky * kz] = np.repeat(self.my, kz, axis=1)
        lane_z[:, 0, : ky * kz] = np.tile(self.mz, (1, ky))
        wave_x = np.zeros((kxp, 128))
        wave_x[:kx] = self.mx[:, None]
        return (
            bf16(t1.reshape(cols * self.modes, self.nz)),
            bf16(t2.reshape(rows, 2 * self.ny, 256)),
            bf16(t3.reshape(2 * kxp, rows * 2 * bx)),
            bf16(t4.reshape(parts, rows * 2 * hx, 2 * kxp)),
            bf16(t5.reshape(rows * 256, 2 * self.ny)),
            bf16(t6.reshape(cols * self.modes, self.nz)),
            f32(wave_x),
            f32(lane_y),
            f32(lane_z),
        )


def whole_kernel(p, fp, factor, cot, feat, win_ref, bin_ref, wmid_ref, bmid_ref, wout_ref,
                    t1, t2, t3, t4, t5, t6, wx_ref, wy_ref, wz_ref,
                    field, o_ref, r_ref, act_in, act_mid,
                    s1, d1, s2, d2, s3, d3, s4, d4, e2, q5, o5, flat, abuf, mbuf,
                    w1_ref, w2_ref, b2_ref, wi_ref, wo_ref, sf_out, sg_out, accm, acci, acco,
                    grads, pair, held, pieces, total, later, gbuf, rest, rest_p, rest_c, rest_z,
                    send1, recv1, send2, recv2, send3, recv3, send4, recv4, sem_a, sem_m,
                    load_a, load_m, send_a, recv_a, send_b, recv_b, send_c, recv_c,
                    send_d, recv_d, send_e, recv_e, send_f, recv_f, send_g, recv_g, sem_g):
    me_r, me_c = lax.axis_index("row"), lax.axis_index("col")
    rows, cols, kz, ky, kxp = p.rows, p.cols, p.kz, p.ky, p.kxp
    bx, by, nc, hx, parts = p.bx, p.by, p.nc, p.hx, p.parts
    last = (((1,), (1,)), ((), ()))
    first = (((0,), (0,)), ((), ()))
    half = jnp.bfloat16

    def row_peer(d):
        return lax.rem(me_r + d, rows)

    def col_peer(d):
        return lax.rem(me_c + d, cols)

    barrier = pltpu.get_barrier_semaphore()
    for d in range(1, rows):
        pl.semaphore_signal(barrier, inc=1, device_id=(row_peer(d), me_c), device_id_type=MESH)
    for d in range(1, cols):
        pl.semaphore_signal(barrier, inc=1, device_id=(me_r, col_peer(d)), device_id_type=MESH)
    layers = rows // 2
    core, me_z = lax.rem(me_r, 2), me_r // 2
    other = (me_r + 1 - 2 * core, me_c)
    share = pieces.shape[1]

    def chip(dz, dc):
        z, c = lax.rem(me_z + dz, layers), lax.rem(me_c + dc, cols)
        return z, c, (2 * z + core, c)

    def place(z, c):
        return pl.ds(pl.multiple_of((z * cols + c) * share, 8), share)

    chips = [(dz, dc) for dz in range(layers) for dc in range(cols) if dz or dc]
    greeted = rows + cols - 2
    for dz, dc in chips:
        if dz and dc:
            greeted += 1
            pl.semaphore_signal(barrier, inc=1, device_id=chip(dz, dc)[2], device_id_type=MESH)
    sends = []

    def over_col(h, src, dst, send, recv):
        copies = []
        for d in range(1, cols):
            copy = pltpu.make_async_remote_copy(
                src_ref=src.at[h, col_peer(d)], dst_ref=dst.at[h, me_c], send_sem=send.at[h, d],
                recv_sem=recv.at[h, d], device_id=(me_r, col_peer(d)), device_id_type=MESH,
            )
            copy.start()
            copies.append(copy)
        dst[h, me_c] = src[h, me_c]
        sends.extend(copies)
        return copies

    def over_row(h, src, dst, send, recv):
        copies = []
        for d in range(1, rows):
            copy = pltpu.make_async_remote_copy(
                src_ref=src.at[h, row_peer(d)], dst_ref=dst.at[h, me_r], send_sem=send.at[h, d],
                recv_sem=recv.at[h, d], device_id=(row_peer(d), me_c), device_id_type=MESH,
            )
            copy.start()
            copies.append(copy)
        dst[h, me_r] = src[h, me_r]
        sends.extend(copies)
        return copies

    def arrived(copies):
        for copy in copies:
            copy.wait_recv()

    steps, hid, block = act_in.shape
    inner = math.gcd(block, 512)
    done = [0]

    def keep(i, slot):
        return (
            pltpu.make_async_copy(
                abuf.at[slot, pl.ds(0, hid)], act_in.at[i], sem_a.at[slot]
            ),
            pltpu.make_async_copy(mbuf.at[slot], act_mid.at[i], sem_m.at[slot]),
        )

    def forward_block(turn, carry):
        slot = lax.rem(turn, 2)
        i = lax.rem(turn + 2, steps)

        @pl.when(turn >= 2)
        def _():
            for copy in keep(i, slot):
                copy.wait()

        src = sf_out[:, pl.ds(pl.multiple_of(i * block, block), block)]
        pre = jnp.dot(w1_ref[...], src, preferred_element_type=jnp.float32)
        act = jnp.tanh(pre).astype(half)
        abuf[slot, pl.ds(0, hid), :] = act
        pre = jnp.dot(w2_ref[...], act, preferred_element_type=jnp.float32) + b2_ref[:, :1]
        mbuf[slot] = jnp.tanh(pre).astype(half)

        @pl.when(turn < steps - 2)
        def _():
            for copy in keep(i, slot):
                copy.start()

        return carry

    def fetch(i, slot):
        return (
            pltpu.make_async_copy(
                act_in.at[i], abuf.at[slot, pl.ds(0, hid)], load_a.at[slot]
            ),
            pltpu.make_async_copy(act_mid.at[i], mbuf.at[slot], load_m.at[slot]),
        )

    later_from = steps // parts if parts > 1 else steps
    wide_inner = math.gcd(block, 2048)

    def put(i, slot):
        return pltpu.make_async_copy(
            gbuf.at[slot], field.at[:, pl.ds(i * (block // 128), block // 128), :], sem_g.at[slot]
        )

    def before_put(i, slot):
        @pl.when(i >= 2)
        def _():
            put(i, slot).wait()

    def finish(i, slot, first_lane, delta, size):
        start = pl.multiple_of(i * block + first_lane, size)
        acci[...] += lax.dot_general(
            sf_out[:, pl.ds(start, size)], delta, last, preferred_element_type=jnp.float32
        )
        grad = jnp.dot(wi_ref[...], delta, preferred_element_type=jnp.float32)
        for row in range(size // 128):
            gbuf[slot, :, first_lane // 128 + row, :] = grad[:fp, row * 128 : (row + 1) * 128]

    def later_block(k, carry):
        i = k + later_from
        slot = lax.rem(i, 2)
        before_put(i, slot)
        for n in range(block // wide_inner):
            delta = later[k, :, pl.ds(n * wide_inner, wide_inner)]
            finish(i, slot, n * wide_inner, delta, wide_inner)
        put(i, slot).start()
        return carry

    def backward_block(defer, i, carry):
        slot = lax.rem(i, 2)
        if not defer:
            before_put(i, slot)

        @pl.when(i >= 2)
        def _():
            for copy in fetch(i, slot):
                copy.wait()

        start = pl.multiple_of(i * block, block)
        abuf[slot, pl.ds(hid, 16), :] = sf_out[:, pl.ds(start, block)]
        back_mid, delta_mid, back_in, delta_in = {}, {}, {}, {}

        def lanes(n):
            return pl.ds(n * inner, inner)

        def source(ref, n):
            return ref[:, pl.ds(pl.multiple_of(start + n * inner, inner), inner)]

        def gate(back, act):
            wide = act.astype(jnp.float32)
            return (back * (1.0 - wide * wide)).astype(half)

        def enter(n):
            sg, act = source(sg_out, n), mbuf[slot, :, lanes(n)]
            acco[...] += lax.dot_general(sg, act, last, preferred_element_type=jnp.float32)
            back_mid[n] = jnp.dot(wo_ref[...], sg, preferred_element_type=jnp.float32)

        def middle(n):
            delta_mid[n] = gate(back_mid.pop(n), mbuf[slot, :, lanes(n)])

        def weigh(n):
            delta = delta_mid.pop(n)
            back_in[n] = jnp.dot(wmid_ref[...], delta, preferred_element_type=jnp.float32)
            accm[...] += lax.dot_general(
                abuf[slot, :, lanes(n)], delta, last, preferred_element_type=jnp.float32
            )

        def lower(n):
            delta_in[n] = gate(back_in.pop(n), abuf[slot, pl.ds(0, hid), lanes(n)])

        def leave(n):
            delta = delta_in.pop(n)
            if defer:
                later[i - later_from, :, lanes(n)] = delta
            else:
                finish(i, slot, n * inner, delta, inner)

        count = block // inner
        for turn in range(count + 4):
            for late, work in ((4, leave), (3, lower), (2, weigh), (1, middle), (0, enter)):
                if 0 <= turn - late < count:
                    work(turn - late)
        if not defer:
            put(i, slot).start()

        @pl.when(i + 2 < steps)
        def _():
            for copy in fetch(i + 2, slot):
                copy.start()

        return carry

    def forward(share):
        upto = min(steps, -(-steps * share // 16))
        if upto > done[0]:
            lax.fori_loop(done[0], upto, forward_block, 0)
            done[0] = upto

    def stage1(h):
        for v in range(nc):
            for g in range(p.hg):
                at = v * p.xg + h * p.hg + g
                a = cot[pl.ds(at * p.wide, p.wide), :].astype(half)
                part = lax.dot_general(t1[...], a, last, preferred_element_type=jnp.float32)
                for c in range(cols):
                    s1[h, c, pl.ds(v * p.hg + g, 2 * kz, stride=p.gp), pl.ds(0, p.wide)] = part[
                        c * p.modes : c * p.modes + 2 * kz
                    ]

    def stage2(h):
        count = kz * p.gp
        where = lax.broadcasted_iota(jnp.int32, (count, 128), 1) // by
        for ri in range(2):
            for j in range(p.xl):
                whole = None
                for c in range(cols):
                    tile = d1[h, c, pl.ds(ri * count, count), :]
                    shift = ((c - j) * by) % 128
                    tile = tile if shift == 0 else pltpu.roll(tile, shift, 1)
                    whole = tile if whole is None else jnp.where(where == c, tile, whole)
                e2[ri, pl.ds(j, count, stride=p.xl), :] = whole
        lhs = jnp.concatenate([e2[0].astype(half), e2[1].astype(half)], axis=1)
        per = p.gp * p.xl
        for r in range(rows):
            part = jnp.dot(lhs, t2[r], preferred_element_type=jnp.float32)
            for ri in range(2):
                total = part[:per, ri * 128 : (ri + 1) * 128]
                for k in range(1, kz):
                    total = total + pltpu.roll(
                        part[k * per : (k + 1) * per, ri * 128 : (ri + 1) * 128], k, 1
                    )
                for v in range(nc):
                    s2[h, r, pl.ds((2 * v + ri) * hx, hx), :] = total[v * hx : (v + 1) * hx]

    def stage3():
        wx, wy, wz = wx_ref[...], wy_ref[me_r], wz_ref[me_c]
        vel = []
        for v in range(nc):
            data = jnp.concatenate(
                [d2[h, r, pl.ds(2 * v * hx, 2 * hx), :] for h in range(parts) for r in range(rows)],
                axis=0,
            )
            hat = jnp.dot(t3[...], data.astype(half), preferred_element_type=jnp.float32)
            vel.append((hat[:kxp], hat[kxp:]))
        inverse = 1.0 / jnp.maximum(wx * wx + wy * wy + wz * wz, 1.0)
        fields = [[], [], [], []]
        for ri in range(2):
            inner = (wx * vel[0][ri] + wy * vel[1][ri] + wz * vel[2][ri]) * inverse
            px = vel[0][ri] - wx * inner
            py = vel[1][ri] - wy * inner
            pz = vel[2][ri] - wz * inner
            fields[0].append(py)
            fields[1].append(pz)
            fields[2].append(wy * px + wx * py)
            fields[3].append(wz * px + wx * pz)
        return [jnp.concatenate(field, axis=0).astype(half) for field in fields]

    def stage4(h, fields):
        for f in range(p.nf):
            part = jnp.dot(t4[h], fields[f], preferred_element_type=jnp.float32)
            for r in range(rows):
                s3[h, r, pl.ds(f * 2 * hx, 2 * hx), :] = part[r * 2 * hx : (r + 1) * 2 * hx]

    def stage5(h):
        span = p.ns * hx
        for r in range(rows):
            wy, wz = wy_ref[r], wz_ref[me_c]
            for ri in range(2):
                qy, qz, xy, xz = [d3[h, r, pl.ds((2 * f + ri) * hx, hx), :] for f in range(p.nf)]
                data = jnp.concatenate([wy * qy, wz * qz, xy, xz, wz * qy + wy * qz], axis=0)
                for k in range(kz):
                    tile = data if k == 0 else pltpu.roll(data, 128 - k, 1)
                    q5[pl.ds(k * span, span), pl.ds((2 * r + ri) * 128, 128)] = tile
        part = jnp.dot(q5[...].astype(half), t5[...], preferred_element_type=jnp.float32)
        for ri in range(2):
            o5[ri] = part[:, ri * 128 : (ri + 1) * 128]
        count = kz * p.sx
        where = lax.broadcasted_iota(jnp.int32, (count, 128), 1) // by
        for ri in range(2):
            tiles = [o5[ri, pl.ds(j, count, stride=p.xl), :] for j in range(p.xl)]
            for c in range(cols):
                whole = None
                for j in range(p.xl):
                    shift = ((j - c) * by) % 128
                    tile = tiles[j] if shift == 0 else pltpu.roll(tiles[j], shift, 1)
                    whole = tile if whole is None else jnp.where(where == j, tile, whole)
                s4[h, c, pl.ds(ri * count, count), :] = whole

    def stage6(h):
        pad = jnp.zeros((p.modes - 2 * kz, 128), jnp.float32)
        for g in range(p.hg):
            comps = []
            for comp in range(p.ns):
                pieces = []
                for c in range(cols):
                    pieces.append(d4[h, c, pl.ds(comp * p.hg + g, 2 * kz, stride=p.sx), :])
                    if p.modes > 2 * kz:
                        pieces.append(pad)
                data = jnp.concatenate(pieces, axis=0).astype(half)
                comps.append(
                    lax.dot_general(data, t6[...], first, preferred_element_type=jnp.float32)[
                        : p.wide
                    ]
                )
            order = [-(comps[0] + comps[1]), comps[0], comps[1], comps[2], comps[3], comps[4]]
            line = (h * p.hg + g) * p.wide
            for comp in range(6):
                flat[pl.ds(line * 16 + comp, p.wide, stride=16), :] = order[comp]
            for n in range(p.wide):
                sg_out[:, pl.ds((line + n) * 128, 128)] = flat[
                    pl.ds((line + n) * 16, 16), :
                ].astype(half)

    def take_weights():
        bias = bin_ref[...]
        high = bias.astype(half).astype(jnp.float32)
        middle = (bias - high).astype(half).astype(jnp.float32)
        low = bias - high - middle
        blank = jnp.zeros((16 - fp - 3, hid), jnp.float32)
        table = jnp.concatenate(
            [win_ref[...].astype(jnp.float32), high, middle, low, blank], axis=0
        )
        w1_ref[...] = table.T.astype(half)
        w2_ref[...] = wmid_ref[...].astype(jnp.float32).T.astype(half)
        b2_ref[...] = jnp.broadcast_to(bmid_ref[...], (128, hid)).T
        outs = wout_ref.shape[0]
        blank = jnp.zeros((16 - fp, hid), jnp.float32)
        wi_ref[...] = jnp.concatenate(
            [win_ref[...].astype(jnp.float32), blank], axis=0
        ).astype(half)
        blank = jnp.zeros((16 - outs, hid), jnp.float32)
        wo_ref[...] = jnp.concatenate(
            [wout_ref[...].astype(jnp.float32), blank], axis=0
        ).T.astype(half)
        accm[...] = jnp.zeros_like(accm)
        acci[...] = jnp.zeros_like(acci)
        acco[...] = jnp.zeros_like(acco)
        if grads.shape[1] > hid:
            grads[...] = jnp.zeros_like(grads)
        rest[...] = jnp.zeros_like(rest)

    def take_features():
        for f in range(16):
            if f < fp:
                value = feat[f].astype(jnp.float32)
            else:
                value = jnp.full((p.lines, 128), 1.0 if f < fp + 3 else 0.0, jnp.float32)
            flat[pl.ds(f, p.lines, stride=16), :] = value
        for n in range(p.lines):
            sf_out[:, pl.ds(n * 128, 128)] = flat[pl.ds(n * 16, 16), :].astype(half)

    if p.wide < 128:
        s1[...] = jnp.zeros_like(s1)
    moves1, moves2, moves3, moves4 = [], [], [], []
    for h in range(parts):
        stage1(h)
        if h == 0:
            pl.semaphore_wait(barrier, greeted)
        moves1.append(over_col(h, s1, d1, send1, recv1))
    take_features()
    take_weights()
    forward(1)
    for h in range(parts):
        arrived(moves1[h])
        stage2(h)
        moves2.append(over_row(h, s2, d2, send2, recv2))
        forward((3, 8)[h])
    for h in range(parts):
        arrived(moves2[h])
    fields = stage3()
    for h in range(parts):
        stage4(h, fields)
        moves3.append(over_row(h, s3, d3, send3, recv3))
        forward((11, 13)[h])
    for h in range(parts):
        arrived(moves3[h])
        stage5(h)
        moves4.append(over_col(h, s4, d4, send4, recv4))
        forward((15, 16)[h])
    forward(16)
    for h in range(parts):
        arrived(moves4[h])
        stage6(h)
        lax.fori_loop(
            steps * h // parts, steps * (h + 1) // parts,
            functools.partial(backward_block, h > 0), 0,
        )
    width = hid // 2
    for side in range(2):
        grads[side, pl.ds(0, hid), :] = accm[pl.ds(0, hid), side * width : (side + 1) * width]
    swap = pltpu.make_async_remote_copy(
        src_ref=grads.at[1 - core], dst_ref=pair, send_sem=send_a, recv_sem=recv_a,
        device_id=other, device_id_type=MESH,
    )
    swap.start()
    left = steps - later_from
    lax.fori_loop(0, left // 8, later_block, 0)
    swap.wait_recv()
    held[...] = grads[core] + pair[...]
    spread, shared, handed, small = [], [], [], []
    for dz, dc in chips:
        z, c, device = chip(dz, dc)
        at = dz * cols + dc
        copy = pltpu.make_async_remote_copy(
            src_ref=held.at[place(z, c)], dst_ref=pieces.at[at], send_sem=send_b.at[at],
            recv_sem=recv_b.at[at], device_id=device, device_id_type=MESH,
        )
        copy.start()
        spread.append(copy)
    lax.fori_loop(left // 8, left, later_block, 0)
    outs = wout_ref.shape[0]
    rest[pl.ds(0, fp + 1), :] = acci[pl.ds(0, fp + 1), :]
    rest[pl.ds(fp + 1, outs), :] = acco[pl.ds(0, outs), :]
    rest[pl.ds(fp + 1 + outs, 1), :] = accm[pl.ds(hid + fp, 1), :]
    trade = pltpu.make_async_remote_copy(
        src_ref=rest, dst_ref=rest_p, send_sem=send_e, recv_sem=recv_e,
        device_id=other, device_id_type=MESH,
    )
    trade.start()
    small.append(trade)
    mine = place(me_z, me_c)
    value = held[mine, :]
    for copy, (dz, dc) in zip(spread, chips):
        copy.wait_recv()
        value = value + pieces[dz * cols + dc]
    total[mine, :] = value * factor

    def hand_over(at, where):
        copy = pltpu.make_async_remote_copy(
            src_ref=total.at[where], dst_ref=o_ref.at[core, where], send_sem=send_d.at[at],
            recv_sem=recv_d.at[at], device_id=other, device_id_type=MESH,
        )
        copy.start()
        handed.append(copy)

    trade.wait_recv()
    rest_c[me_c] = rest[...] + rest_p[...]
    moves = []
    for dc in range(1, cols):
        copy = pltpu.make_async_remote_copy(
            src_ref=rest_c.at[me_c], dst_ref=rest_c.at[me_c], send_sem=send_f.at[dc],
            recv_sem=recv_f.at[dc], device_id=(me_r, col_peer(dc)), device_id_type=MESH,
        )
        copy.start()
        moves.append(copy)
    small.extend(moves)
    for dz, dc in chips:
        at = dz * cols + dc
        copy = pltpu.make_async_remote_copy(
            src_ref=total.at[mine], dst_ref=total.at[mine], send_sem=send_c.at[at],
            recv_sem=recv_c.at[at], device_id=chip(dz, dc)[2], device_id_type=MESH,
        )
        copy.start()
        shared.append(copy)
    hand_over(0, mine)
    arrived(moves)
    value = rest_c[0]
    for c in range(1, cols):
        value = value + rest_c[c]
    rest_z[me_z] = value
    moves = []
    for dz in range(1, layers):
        copy = pltpu.make_async_remote_copy(
            src_ref=rest_z.at[me_z], dst_ref=rest_z.at[me_z], send_sem=send_g.at[dz],
            recv_sem=recv_g.at[dz], device_id=chip(dz, 0)[2], device_id_type=MESH,
        )
        copy.start()
        moves.append(copy)
    small.extend(moves)
    for copy, (dz, dc) in zip(shared, chips):
        copy.wait_recv()
        z, c, _ = chip(layers - dz, cols - dc)
        hand_over(dz * cols + dc, place(z, c))
    arrived(moves)
    value = rest_z[0]
    for z in range(1, layers):
        value = value + rest_z[z]
    r_ref[...] = value * factor
    o_ref[core] = total[...]
    arrived(handed)
    for i in range(max(0, steps - 2), steps):
        put(i, i % 2).wait()
    for copy in sends + [swap] + spread + shared + handed + small:
        copy.wait_send()


def whole(features, cotangent, w_in, bias_in, w_mid, bias_mid, w_out, rows, cols):
    p = Plan(cotangent.shape, rows, cols)
    feat, hid = w_in.shape
    cells = p.lines * p.nz
    block = math.gcd(cells, 4096)
    steps = cells // block
    count = rows // 2 * cols
    length = up(hid, 8 * count)
    few = up(feat + 2 + w_out.shape[1], 8)
    layers = rows // 2
    factor = 1.0 / math.sqrt(cells * rows * cols)
    dma = pltpu.SemaphoreType.DMA
    vmem = pl.BlockSpec(memory_space=pltpu.VMEM)
    hbm = pl.BlockSpec(memory_space=pl.ANY)
    single, half = jnp.float32, jnp.bfloat16
    parts = p.parts
    buffer = pltpu.VMEM((length, hid // 2), single)
    field, total, rest, _, _ = pl.pallas_call(
        functools.partial(whole_kernel, p, feat, factor),
        out_shape=[
            jax.ShapeDtypeStruct((feat, p.lines, p.nz), single),
            jax.ShapeDtypeStruct((2, length, hid // 2), single),
            jax.ShapeDtypeStruct((few, hid), single),
            jax.ShapeDtypeStruct((steps, hid, block), half),
            jax.ShapeDtypeStruct((steps, hid, block), half),
        ],
        in_specs=[vmem] * 16,
        out_specs=[hbm, vmem, vmem, hbm, hbm],
        scratch_shapes=[
            pltpu.VMEM((parts, cols, p.rows1, 128), single),
            pltpu.VMEM((parts, cols, p.rows1, 128), single),
            pltpu.VMEM((parts, rows, p.rows2, 128), single),
            pltpu.VMEM((parts, rows, p.rows2, 128), single),
            pltpu.VMEM((parts, rows, p.rows3, 128), single),
            pltpu.VMEM((parts, rows, p.rows3, 128), single),
            pltpu.VMEM((parts, cols, p.rows4, 128), single),
            pltpu.VMEM((parts, cols, p.rows4, 128), single),
            pltpu.VMEM((2, p.kz * p.gp * p.xl, 128), single),
            pltpu.VMEM((p.kz * p.ns * p.hx, rows * 256), single),
            pltpu.VMEM((2, p.kz * p.ns * p.hx, 128), single),
            pltpu.VMEM((p.lines * 16, 128), single),
            pltpu.VMEM((2, hid + 16, block), half),
            pltpu.VMEM((2, hid, block), half),
            pltpu.VMEM((hid, 16), half),
            pltpu.VMEM((hid, hid), half),
            pltpu.VMEM((hid, 128), single),
            pltpu.VMEM((16, hid), half),
            pltpu.VMEM((hid, 16), half),
            pltpu.VMEM((16, cells), half),
            pltpu.VMEM((16, cells), half),
            pltpu.VMEM((hid + 16, hid), single),
            pltpu.VMEM((16, hid), single),
            pltpu.VMEM((16, hid), single),
            pltpu.VMEM((2, length, hid // 2), single),
            buffer,
            buffer,
            pltpu.VMEM((count, length // count, hid // 2), single),
            buffer,
            pltpu.VMEM((max(1, steps - steps // parts), hid, block), half),
            pltpu.VMEM((2, feat, block // 128, 128), single),
            pltpu.VMEM((few, hid), single),
            pltpu.VMEM((few, hid), single),
            pltpu.VMEM((cols, few, hid), single),
            pltpu.VMEM((layers, few, hid), single),
            dma((parts, cols)), dma((parts, cols)), dma((parts, rows)), dma((parts, rows)),
            dma((parts, rows)), dma((parts, rows)), dma((parts, cols)), dma((parts, cols)),
            dma((2,)), dma((2,)), dma((2,)), dma((2,)),
            dma(()), dma(()), dma((count,)), dma((count,)), dma((count,)), dma((count,)),
            dma((count,)), dma((count,)),
            dma(()), dma(()), dma((cols,)), dma((cols,)), dma((layers,)), dma((layers,)), dma((2,)),
        ],
        compiler_params=pltpu.CompilerParams(
            collective_id=1, has_side_effects=True, vmem_limit_bytes=58 << 20
        ),
        name="whole",
    )(
        cotangent.reshape(p.nc * p.lines, p.nz), features.reshape(feat, p.lines, p.nz),
        w_in, bias_in[None], w_mid, bias_mid[None], w_out.T, *p.tables(),
    )
    return field, total, rest


def final_kernel(feat, outs, f_ref, t_ref, r_ref,
                 field_ref, win_ref, bin_ref, wmid_ref, bmid_ref, wout_ref,
                 held, wide, into, away, side_in, side_out):
    arrive = [pltpu.make_async_copy(f_ref.at[f], held.at[f], into.at[f]) for f in range(feat)]
    depart = [pltpu.make_async_copy(held.at[f], field_ref.at[f], away.at[f]) for f in range(feat)]
    for copy in arrive:
        copy.start()
    hid = wmid_ref.shape[0]
    side = hid // 2
    inward = [
        pltpu.make_async_copy(t_ref.at[n, pl.ds(0, hid)], wide.at[n], side_in.at[n])
        for n in range(2)
    ]
    outward = [
        pltpu.make_async_copy(
            wide.at[n], wmid_ref.at[:, pl.ds(n * side, side)], side_out.at[n]
        )
        for n in range(2)
    ]
    for copy in inward:
        copy.start()
    win_ref[...] = r_ref[pl.ds(0, feat), :]
    bin_ref[...] = r_ref[pl.ds(feat, 1), :]
    wout_ref[...] = r_ref[pl.ds(feat + 1, outs), :]
    bmid_ref[...] = r_ref[pl.ds(feat + 1 + outs, 1), :]
    for coming, going in zip(arrive + inward, depart + outward):
        coming.wait()
        going.start()
    for copy in depart + outward:
        copy.wait()


def final(field, total, rest, feat, outs, hid):
    vmem = pl.BlockSpec(memory_space=pltpu.VMEM)
    hbm = pl.BlockSpec(memory_space=pl.ANY)
    single = jnp.float32
    return pl.pallas_call(
        functools.partial(final_kernel, feat, outs),
        out_shape=[
            jax.ShapeDtypeStruct(field.shape, single),
            jax.ShapeDtypeStruct((feat, hid), single),
            jax.ShapeDtypeStruct((1, hid), single),
            jax.ShapeDtypeStruct((hid, hid), single),
            jax.ShapeDtypeStruct((1, hid), single),
            jax.ShapeDtypeStruct((outs, hid), single),
        ],
        in_specs=[hbm, hbm, vmem],
        out_specs=[hbm, vmem, vmem, hbm, vmem, vmem],
        scratch_shapes=[
            pltpu.VMEM(field.shape, single),
            pltpu.VMEM((2, hid, hid // 2), single),
            pltpu.SemaphoreType.DMA((feat,)),
            pltpu.SemaphoreType.DMA((feat,)),
            pltpu.SemaphoreType.DMA((2,)),
            pltpu.SemaphoreType.DMA((2,)),
        ],
        name="final",
    )(field, total, rest)


def per_device(features, cotangent, w_in, bias_in, w_mid, bias_mid, w_out, rows, cols):
    field, total, rest = whole(
        features, cotangent, w_in, bias_in, w_mid, bias_mid, w_out, rows, cols
    )
    field, g_in, b_in, g_mid, b_mid, g_out = final(
        field, total, rest, features.shape[0], w_out.shape[1], len(w_mid)
    )
    return field.reshape(features.shape), g_in, b_in[0], g_mid, b_mid[0], g_out.T


def solution(mesh):
    body = functools.partial(per_device, rows=mesh.shape["row"], cols=mesh.shape["col"])
    return jax.shard_map(
        body,
        mesh=mesh,
        in_specs=(
            P(None, None, "row", "col", None),
            P(None, None, "row", "col", None),
            P(),
            P(),
            P(),
            P(),
            P(),
        ),
        out_specs=(P(None, None, "row", "col", None), P(), P(), P(), P(), P()),
        check_vma=False,
    )
```
